128 devices in a mesh: row: 4 (over y_lo, core), col: 32 (over x, z, y_hi).
Axes of the slice: x: 4, y: 4 (y_hi: 2, y_lo: 2; y = y_hi * 2 + y_lo), z: 4, core: 2. Of those that a mesh axis runs over, the one named last changes fastest.
Arguments:
- features: bfloat16 [65536, 256], P(('row', 'col')), may hold values from -6 to 6
- tile_values: bfloat16 [256, 64, 256, 256], P('col', 'row'), may hold values from 0 to 1, as said below
- tile_cols: int32 [256, 64], P('col', 'row'), may hold values from 0 to 63
- tile_counts: int32 [256, 4], P('col', 'row'), may hold values from 1 to 16, as said below
- weight: bfloat16 [256, 256], replicated, may hold values from -0.375 to 0.375
- bias: float32 [256], replicated, may hold values from -3 to 3
- cotangent: bfloat16 [65536, 256], P(('col', 'row')), may hold values from -6 to 6
Outputs:
- layer_out: bfloat16 [65536, 256], P(('col', 'row'))
- feature_grad: bfloat16 [65536, 256], P(('row', 'col'))
- weight_grad: float32 [256, 256], replicated
- bias_grad: float32 [256], replicated
The draws below stay inside these ranges and needn't reach their ends.
Inputs may be any that keep to these rules, and one draw needn't show every extreme that they name: `tile_values`: nonnegative edge weights. `tile_counts`: every draw has some entry equal to 16; the loads differ between the devices' blocks.
All inputs are finite; a program needn't handle non-finite values.
Results may differ from the reference program's by a relative error of at most 0.025.
Values may be sent and summed in bfloat16 or wider, within the bound.
A program may use at most 128 MiB of HBM per device.

```python
import math
import jax
import jax.numpy as jnp
from jax import lax

HID = 256
TILE = 256
SLOTS = 16
NODES = 65536
ROW_TILES = 8
COL_TILES = 64
N_ROW = 4
N_COL = 32


def draw_tile_values(key, part):
    shape = (N_COL * ROW_TILES, N_ROW * SLOTS, TILE, TILE)
    spread = (3.0 / (N_ROW * SLOTS * TILE)) ** 0.5
    values = jax.random.uniform(key, shape, jnp.float32, 0.0, 1.0) * spread
    return values.astype(jnp.bfloat16)


def draw_tile_counts(key, part):
    level_key = jax.random.fold_in(key, 11)
    count_key = jax.random.fold_in(key, 12)
    place_key = jax.random.fold_in(key, 13)
    levels = jax.random.randint(level_key, (N_COL, N_ROW), 0, 4)
    limits = jnp.maximum(1, SLOTS // 2 ** levels)
    limits = jnp.repeat(limits, ROW_TILES, axis=0)
    counts = jax.random.randint(count_key, (N_COL * ROW_TILES, N_ROW), 1, limits + 1)
    chosen = jax.random.randint(place_key, (), 0, N_COL * ROW_TILES * N_ROW)
    flat_iota = jnp.arange(N_COL * ROW_TILES * N_ROW, dtype=jnp.int32).reshape(N_COL * ROW_TILES, N_ROW)
    counts = jnp.where(flat_iota == chosen, SLOTS, counts)
    return counts.astype(jnp.int32)


def with_ends(values, rng, smallest, high):
    index_at = [jax.random.randint(jax.random.fold_in(rng, axis), (), 0, length) for axis, length in enumerate(values.shape)]
    longest = values.shape.index(max(values.shape))
    next_to = index_at[:longest] + [(index_at[longest] + 1) % values.shape[longest]] + index_at[longest + 1:]
    return values.at[tuple(index_at)].set(smallest).at[tuple(next_to)].set(high)


def block_scale(key, shape, cuts, low, high):
    level, own = 1.0, jax.random.fold_in(key, 6)
    for dim, shards_of in cuts:
        steps = jnp.exp(jax.random.uniform(jax.random.fold_in(own, dim), (shards_of,), jnp.float32, low / len(cuts), high / len(cuts)))
        level = level * jnp.repeat(steps, shape[dim] // shards_of).reshape([-1 if axis == dim else 1 for axis in range(len(shape))])
    return level


def scatter_about(own_key, extent, width, limit, pieces=(), kind=jnp.bfloat16):
    array = jax.random.normal(own_key, extent, jnp.float32) * width
    if len(pieces) > 0:
        array = block_scale(own_key, extent, pieces, -0.22, 0.18) * array
    return jnp.clip(array, min=-limit, max=limit).astype(kind)


def setup_inputs(seed: int = 0) -> dict:
    streams_of = jax.random.split(jax.random.key(seed), 8)
    return {
        "features": scatter_about(streams_of[0], (NODES, HID), 1.0, 6.0, ((0, 128),)),
        "tile_values": draw_tile_values(jax.random.fold_in(streams_of[7], 71), 0),
        "tile_cols": with_ends(jax.random.randint(streams_of[2], (N_COL * ROW_TILES, N_ROW * SLOTS), 0, COL_TILES), jax.random.fold_in(streams_of[2], 1), 0, COL_TILES - 1).astype(jnp.int32),
        "tile_counts": draw_tile_counts(jax.random.fold_in(streams_of[7], 71), 0),
        "weight": scatter_about(streams_of[4], (HID, HID), HID ** -0.5, 0.375),
        "bias": scatter_about(streams_of[5], (HID,), 0.5, 3.0, (), jnp.float32),
        "cotangent": scatter_about(streams_of[6], (NODES, HID), 1.0, 6.0, ((0, 128),)),
    }


def reference(features, tile_values, tile_cols, tile_counts, weight, bias, cotangent):
    node_total = features.shape[0]
    x_tiles = features.reshape(node_total // TILE, TILE, HID)
    slot_iota = jnp.arange(N_ROW * SLOTS, dtype=jnp.int32)
    source_block = (slot_iota // SLOTS).astype(jnp.int32)
    within_block = (slot_iota % SLOTS).astype(jnp.int32)

    def tile_meta(tile_index):
        source_index = (source_block * COL_TILES + tile_cols[tile_index]).astype(jnp.int32)
        active = (within_block < tile_counts[tile_index][source_block]).astype(jnp.float32)
        return (source_index, active)

    def forward_tile(tile_index):
        source_index, active = tile_meta(tile_index)
        picked = x_tiles[source_index].astype(jnp.float32) * active[:, None, None]
        return jnp.einsum('kij,kjf->if', tile_values[tile_index].astype(jnp.float32), picked)
    tile_range = jnp.arange(N_COL * ROW_TILES, dtype=jnp.int32)
    hidden = lax.map(forward_tile, tile_range).reshape(node_total, HID).astype(jnp.bfloat16)
    preact = jnp.dot(hidden, weight, preferred_element_type=jnp.float32) + bias
    layer_out = jax.nn.silu(preact).astype(jnp.bfloat16)
    sigmoid_value = jax.nn.sigmoid(preact)
    slope = sigmoid_value * (1.0 + preact * (1.0 - sigmoid_value))
    preact_grad = (cotangent.astype(jnp.float32) * slope).astype(jnp.bfloat16)
    grad_scale = 1.0 / math.sqrt(node_total)
    weight_grad = lax.dot_general(hidden, preact_grad, (((0,), (0,)), ((), ())), preferred_element_type=jnp.float32) * grad_scale
    bias_grad = lax.optimization_barrier(jnp.sum(preact_grad.astype(jnp.float32), axis=0)) * grad_scale
    hidden_grad = lax.dot_general(preact_grad, weight, (((1,), (1,)), ((), ())), preferred_element_type=jnp.float32).astype(jnp.bfloat16)
    grad_tiles = hidden_grad.reshape(node_total // TILE, TILE, HID)

    def back_step(running, tile_index):
        source_index, active = tile_meta(tile_index)
        contrib = jnp.einsum('kij,if->kjf', tile_values[tile_index].astype(jnp.float32), grad_tiles[tile_index].astype(jnp.float32))
        contrib = contrib * active[:, None, None]
        return (running.at[source_index].add(contrib), None)
    start_value = jnp.zeros((node_total // TILE, TILE, HID), jnp.float32)
    summed, _ = lax.scan(back_step, start_value, tile_range)
    feature_grad = summed.reshape(node_total, HID).astype(jnp.bfloat16)
    return (layer_out, feature_grad, weight_grad, bias_grad)
```

```python
import functools
import math

import jax
import jax.numpy as jnp
from jax import lax
from jax.experimental import pallas as pl
from jax.experimental.pallas import tpu as pltpu
from jax.sharding import PartitionSpec as P

VMEM_LIMIT = 60 * 1024 * 1024


def forward_kernel(cols_ref, counts_ref, a_ref, x_ref, o_ref, acc_ref):
    t = pl.program_id(0)
    slots = a_ref.shape[1]
    last = x_ref.shape[0] - 1
    live = jnp.clip(counts_ref[t], 0, slots)
    acc_ref[...] = jnp.zeros_like(acc_ref)

    def body(s, carry):
        j = jnp.clip(cols_ref[t, s], 0, last)
        acc_ref[...] += jnp.dot(a_ref[0, s], x_ref[j], preferred_element_type=jnp.float32)
        return carry

    lax.fori_loop(0, live, body, 0)
    o_ref[0] = acc_ref[...].astype(o_ref.dtype)


def backward_kernel(cols_ref, counts_ref, a_ref, g_ref, o_ref, acc_ref):
    t = pl.program_id(0)
    slots = a_ref.shape[1]
    last = acc_ref.shape[0] - 1
    live = jnp.clip(counts_ref[t], 0, slots)

    @pl.when(t == 0)
    def _():
        acc_ref[...] = jnp.zeros_like(acc_ref)

    g = g_ref[0]

    def body(s, carry):
        j = jnp.clip(cols_ref[t, s], 0, last)
        acc_ref[j] += lax.dot_general(
            a_ref[0, s], g, (((0,), (0,)), ((), ())), preferred_element_type=jnp.float32
        )
        return carry

    lax.fori_loop(0, live, body, 0)

    @pl.when(t == pl.num_programs(0) - 1)
    def _():
        def put(j, carry):
            o_ref[j] = acc_ref[j].astype(o_ref.dtype)
            return carry

        lax.fori_loop(0, acc_ref.shape[0], put, 0)


def aggregate(tile_values, cols, counts, x_tiles):
    row_tiles, slots, tile, _ = tile_values.shape
    col_tiles, _, width = x_tiles.shape
    return pl.pallas_call(
        forward_kernel,
        out_shape=jax.ShapeDtypeStruct((row_tiles, tile, width), jnp.bfloat16),
        grid_spec=pltpu.PrefetchScalarGridSpec(
            num_scalar_prefetch=2,
            grid=(row_tiles,),
            in_specs=[
                pl.BlockSpec((1, slots, tile, tile), lambda t, c, n: (t, 0, 0, 0)),
                pl.BlockSpec(
                    (col_tiles, tile, width),
                    lambda t, c, n: (0, 0, 0),
                    pipeline_mode=pl.Buffered(1),
                ),
            ],
            out_specs=pl.BlockSpec((1, tile, width), lambda t, c, n: (t, 0, 0)),
            scratch_shapes=[pltpu.VMEM((tile, width), jnp.float32)],
        ),
        compiler_params=pltpu.CompilerParams(vmem_limit_bytes=VMEM_LIMIT),
    )(cols, counts, tile_values, x_tiles)


def aggregate_transposed(tile_values, cols, counts, g_tiles, col_tiles):
    row_tiles, slots, tile, _ = tile_values.shape
    width = g_tiles.shape[-1]
    return pl.pallas_call(
        backward_kernel,
        out_shape=jax.ShapeDtypeStruct((col_tiles, tile, width), jnp.bfloat16),
        grid_spec=pltpu.PrefetchScalarGridSpec(
            num_scalar_prefetch=2,
            grid=(row_tiles,),
            in_specs=[
                pl.BlockSpec((1, slots, tile, tile), lambda t, c, n: (t, 0, 0, 0)),
                pl.BlockSpec((1, tile, width), lambda t, c, n: (t, 0, 0)),
            ],
            out_specs=pl.BlockSpec((col_tiles, tile, width), lambda t, c, n: (0, 0, 0)),
            scratch_shapes=[pltpu.VMEM((col_tiles, tile, width), jnp.float32)],
        ),
        compiler_params=pltpu.CompilerParams(vmem_limit_bytes=VMEM_LIMIT),
    )(cols, counts, tile_values, g_tiles)


def gather_over(x, axis):
    size = lax.axis_size(axis)
    spread = jnp.broadcast_to(x[None], (size,) + x.shape)
    got = lax.all_to_all(spread, axis, 0, 0, tiled=True)
    return got.reshape((size * x.shape[0],) + x.shape[1:])


def sum_scatter_over(x, axis):
    size = lax.axis_size(axis)
    parts = x.reshape((size, x.shape[0] // size) + x.shape[1:])
    got = lax.all_to_all(parts, axis, 0, 0, tiled=True)
    return got.astype(jnp.float32).sum(axis=0)


def dense_part(hidden, weight, bias, cotangent):
    preact = jnp.dot(hidden, weight, preferred_element_type=jnp.float32) + bias
    output = jax.nn.silu(preact).astype(jnp.bfloat16)
    sigmoid_value = jax.nn.sigmoid(preact)
    slope = sigmoid_value * (1.0 + preact * (1.0 - sigmoid_value))
    preact_grad = (cotangent.astype(jnp.float32) * slope).astype(jnp.bfloat16)
    weight_grad = lax.dot_general(
        hidden, preact_grad, (((0,), (0,)), ((), ())), preferred_element_type=jnp.float32
    )
    bias_grad = jnp.sum(preact_grad.astype(jnp.float32), axis=0)
    hidden_grad = lax.dot_general(
        preact_grad, weight, (((1,), (1,)), ((), ())), preferred_element_type=jnp.float32
    ).astype(jnp.bfloat16)
    return (output, weight_grad, bias_grad, hidden_grad)


def all_sum(weight_grad, bias_grad):
    axes = ("row", "col")
    devices = lax.axis_size("row") * lax.axis_size("col")
    width = weight_grad.shape[1]
    rows = weight_grad.shape[0] + 1
    per = -(-rows // devices)
    packed = jnp.concatenate(
        [weight_grad, bias_grad[None], jnp.zeros((per * devices - rows, width), jnp.float32)]
    )
    parts = lax.all_to_all(packed.reshape(devices, per, width), axes, 0, 0, tiled=True)
    summed = parts.sum(axis=0, keepdims=True)
    spread = jnp.broadcast_to(summed, (devices, per, width))
    back = lax.all_to_all(spread, axes, 0, 0, tiled=True).reshape(devices * per, width)
    return back[: rows - 1], back[rows - 1]


def per_device(features, tile_values, tile_cols, tile_counts, weight, bias, cotangent):
    node_dev, width = features.shape
    row_tiles, slot_count, tile_size, _ = tile_values.shape
    column_block = gather_over(features, "col")
    column_tiles = column_block.shape[0] // tile_size
    x_tiles = column_block.reshape(column_tiles, tile_size, width)
    live_counts = tile_counts[:, 0]

    partial_value = aggregate(tile_values, tile_cols, live_counts, x_tiles)
    partial_value = partial_value.reshape(row_tiles * tile_size, width)
    node_total = node_dev * lax.axis_size("row") * lax.axis_size("col")
    grad_scale = 1.0 / math.sqrt(node_total)
    own_rows = sum_scatter_over(partial_value, "row").astype(jnp.bfloat16)
    layer_out, weight_grad, bias_grad, hidden_grad = dense_part(own_rows, weight, bias, cotangent)
    weight_grad, bias_grad = all_sum(weight_grad, bias_grad)
    grad_block = gather_over(hidden_grad, "row")
    grad_tiles = grad_block.reshape(row_tiles, tile_size, width)

    summed = aggregate_transposed(tile_values, tile_cols, live_counts, grad_tiles, column_tiles)
    summed = summed.reshape(column_tiles * tile_size, width)
    feature_grad = sum_scatter_over(summed, "col").astype(jnp.bfloat16)
    return (layer_out, feature_grad, weight_grad * grad_scale, bias_grad * grad_scale)


def solution(mesh):
    placed = (
        P(("row", "col"), None),
        P("col", "row", None, None),
        P("col", "row"),
        P("col", "row"),
        P(),
        P(),
        P(("col", "row"), None),
    )
    return jax.shard_map(
        per_device,
        mesh=mesh,
        in_specs=placed,
        out_specs=(P(("col", "row"), None), P(("row", "col"), None), P(), P()),
        check_vma=False,
    )
```

```python
import functools
import math

import jax
import jax.numpy as jnp
from jax import lax
from jax.experimental import pallas as pl
from jax.experimental.pallas import tpu as pltpu
from jax.sharding import PartitionSpec as P

VMEM_LIMIT = 60 * 1024 * 1024


def forward_kernel(cols_ref, counts_ref, a_ref, x_ref, o_ref, acc_ref):
    t = pl.program_id(0)
    slots = a_ref.shape[1]
    last = x_ref.shape[0] - 1
    live = jnp.clip(counts_ref[t], 0, slots)
    acc_ref[...] = jnp.zeros_like(acc_ref)

    def body(s, carry):
        j = jnp.clip(cols_ref[t, s], 0, last)
        acc_ref[...] += jnp.dot(a_ref[0, s], x_ref[j], preferred_element_type=jnp.float32)
        return carry

    lax.fori_loop(0, live, body, 0)
    o_ref[0] = acc_ref[...].astype(o_ref.dtype)


def backward_kernel(cols_ref, counts_ref, a_ref, g_ref, o_ref, acc_ref):
    t = pl.program_id(0)
    slots = a_ref.shape[1]
    last = acc_ref.shape[0] - 1
    live = jnp.clip(counts_ref[t], 0, slots)

    @pl.when(t == 0)
    def _():
        acc_ref[...] = jnp.zeros_like(acc_ref)

    g = g_ref[0]

    def body(s, carry):
        j = jnp.clip(cols_ref[t, s], 0, last)
        acc_ref[j] += lax.dot_general(
            a_ref[0, s], g, (((0,), (0,)), ((), ())), preferred_element_type=jnp.float32
        )
        return carry

    lax.fori_loop(0, live, body, 0)

    @pl.when(t == pl.num_programs(0) - 1)
    def _():
        def put(j, carry):
            o_ref[j] = acc_ref[j].astype(o_ref.dtype)
            return carry

        lax.fori_loop(0, acc_ref.shape[0], put, 0)


def aggregate(tile_values, cols, counts, x_tiles):
    row_tiles, slots, tile, _ = tile_values.shape
    col_tiles, _, width = x_tiles.shape
    return pl.pallas_call(
        forward_kernel,
        out_shape=jax.ShapeDtypeStruct((row_tiles, tile, width), jnp.bfloat16),
        grid_spec=pltpu.PrefetchScalarGridSpec(
            num_scalar_prefetch=2,
            grid=(row_tiles,),
            in_specs=[
                pl.BlockSpec((1, slots, tile, tile), lambda t, c, n: (t, 0, 0, 0)),
                pl.BlockSpec(
                    (col_tiles, tile, width),
                    lambda t, c, n: (0, 0, 0),
                    pipeline_mode=pl.Buffered(1),
                ),
            ],
            out_specs=pl.BlockSpec((1, tile, width), lambda t, c, n: (t, 0, 0)),
            scratch_shapes=[pltpu.VMEM((tile, width), jnp.float32)],
        ),
        compiler_params=pltpu.CompilerParams(vmem_limit_bytes=VMEM_LIMIT),
    )(cols, counts, tile_values, x_tiles)


def aggregate_transposed(tile_values, cols, counts, g_tiles, col_tiles):
    row_tiles, slots, tile, _ = tile_values.shape
    width = g_tiles.shape[-1]
    return pl.pallas_call(
        backward_kernel,
        out_shape=jax.ShapeDtypeStruct((col_tiles, tile, width), jnp.bfloat16),
        grid_spec=pltpu.PrefetchScalarGridSpec(
            num_scalar_prefetch=2,
            grid=(row_tiles,),
            in_specs=[
                pl.BlockSpec((1, slots, tile, tile), lambda t, c, n: (t, 0, 0, 0)),
                pl.BlockSpec((1, tile, width), lambda t, c, n: (t, 0, 0)),
            ],
            out_specs=pl.BlockSpec((col_tiles, tile, width), lambda t, c, n: (0, 0, 0)),
            scratch_shapes=[pltpu.VMEM((col_tiles, tile, width), jnp.float32)],
        ),
        compiler_params=pltpu.CompilerParams(vmem_limit_bytes=VMEM_LIMIT),
    )(cols, counts, tile_values, g_tiles)


def gather_over(x, axis):
    size = lax.axis_size(axis)
    spread = jnp.broadcast_to(x[None], (size,) + x.shape)
    got = lax.all_to_all(spread, axis, 0, 0, tiled=True)
    return got.reshape((size * x.shape[0],) + x.shape[1:])


def sum_scatter_over(x, axis):
    size = lax.axis_size(axis)
    parts = x.reshape((size, x.shape[0] // size) + x.shape[1:])
    got = lax.all_to_all(parts, axis, 0, 0, tiled=True)
    return got.astype(jnp.float32).sum(axis=0)


def dense_part(hidden, weight, bias, cotangent):
    preact = jnp.dot(hidden, weight, preferred_element_type=jnp.float32) + bias
    output = jax.nn.silu(preact).astype(jnp.bfloat16)
    sigmoid_value = jax.nn.sigmoid(preact)
    slope = sigmoid_value * (1.0 + preact * (1.0 - sigmoid_value))
    preact_grad = (cotangent.astype(jnp.float32) * slope).astype(jnp.bfloat16)
    weight_grad = lax.dot_general(
        hidden, preact_grad, (((0,), (0,)), ((), ())), preferred_element_type=jnp.float32
    )
    bias_grad = jnp.sum(preact_grad.astype(jnp.float32), axis=0)
    hidden_grad = lax.dot_general(
        preact_grad, weight, (((1,), (1,)), ((), ())), preferred_element_type=jnp.float32
    ).astype(jnp.bfloat16)
    return (output, weight_grad, bias_grad, hidden_grad)


def per_device(features, tile_values, tile_cols, tile_counts, weight, bias, cotangent):
    node_dev, width = features.shape
    row_tiles, slot_count, tile_size, _ = tile_values.shape
    column_block = gather_over(features, "col")
    column_tiles = column_block.shape[0] // tile_size
    x_tiles = column_block.reshape(column_tiles, tile_size, width)
    live_counts = tile_counts[:, 0]

    partial_value = aggregate(tile_values, tile_cols, live_counts, x_tiles)
    partial_value = partial_value.reshape(row_tiles * tile_size, width)
    node_total = node_dev * lax.axis_size("row") * lax.axis_size("col")
    grad_scale = 1.0 / math.sqrt(node_total)
    own_rows = sum_scatter_over(partial_value, "row").astype(jnp.bfloat16)
    layer_out, weight_grad, bias_grad, hidden_grad = dense_part(own_rows, weight, bias, cotangent)
    packed = lax.psum(jnp.concatenate([weight_grad, bias_grad[None]]), ("row", "col"))
    weight_grad, bias_grad = packed[:-1], packed[-1]
    grad_block = gather_over(hidden_grad, "row")
    grad_tiles = grad_block.reshape(row_tiles, tile_size, width)

    summed = aggregate_transposed(tile_values, tile_cols, live_counts, grad_tiles, column_tiles)
    summed = summed.reshape(column_tiles * tile_size, width)
    feature_grad = sum_scatter_over(summed, "col").astype(jnp.bfloat16)
    return (layer_out, feature_grad, weight_grad * grad_scale, bias_grad * grad_scale)


def solution(mesh):
    placed = (
        P(("row", "col"), None),
        P("col", "row", None, None),
        P("col", "row"),
        P("col", "row"),
        P(),
        P(),
        P(("col", "row"), None),
    )
    return jax.shard_map(
        per_device,
        mesh=mesh,
        in_specs=placed,
        out_specs=(P(("col", "row"), None), P(("row", "col"), None), P(), P()),
        check_vma=False,
    )
```

```python
import functools
import math

import jax
import jax.numpy as jnp
from jax import lax
from jax.experimental import pallas as pl
from jax.experimental.pallas import tpu as pltpu
from jax.sharding import PartitionSpec as P

VMEM_LIMIT = 60 * 1024 * 1024


def forward_kernel(cols_ref, counts_ref, a_ref, x_ref, o_ref):
    t = pl.program_id(0)
    slots = a_ref.shape[1]
    last = x_ref.shape[0] - 1
    live = counts_ref[t]
    acc = None
    for s in range(slots):
        j = jnp.clip(cols_ref[t, s], 0, last)
        term = jnp.dot(a_ref[0, s], x_ref[j], preferred_element_type=jnp.float32)
        term = jnp.where(s < live, term, 0.0)
        acc = term if acc is None else acc + term
    o_ref[0] = acc.astype(o_ref.dtype)


def backward_kernel(cols_ref, counts_ref, a_ref, g_ref, o_ref, acc_ref):
    t = pl.program_id(0)
    slots = a_ref.shape[1]
    last = acc_ref.shape[0] - 1
    live = counts_ref[t]

    @pl.when(t == 0)
    def _():
        acc_ref[...] = jnp.zeros_like(acc_ref)

    g = g_ref[0]
    for s in range(slots):
        j = jnp.clip(cols_ref[t, s], 0, last)
        term = lax.dot_general(
            a_ref[0, s], g, (((0,), (0,)), ((), ())), preferred_element_type=jnp.float32
        )
        acc_ref[j] += jnp.where(s < live, term, 0.0)

    @pl.when(t == pl.num_programs(0) - 1)
    def _():
        def put(j, carry):
            o_ref[j] = acc_ref[j].astype(o_ref.dtype)
            return carry

        lax.fori_loop(0, acc_ref.shape[0], put, 0)


def aggregate(tile_values, cols, counts, x_tiles):
    row_tiles, slots, tile, _ = tile_values.shape
    col_tiles, _, width = x_tiles.shape
    return pl.pallas_call(
        forward_kernel,
        out_shape=jax.ShapeDtypeStruct((row_tiles, tile, width), jnp.bfloat16),
        grid_spec=pltpu.PrefetchScalarGridSpec(
            num_scalar_prefetch=2,
            grid=(row_tiles,),
            in_specs=[
                pl.BlockSpec((1, slots, tile, tile), lambda t, c, n: (t, 0, 0, 0)),
                pl.BlockSpec(
                    (col_tiles, tile, width),
                    lambda t, c, n: (0, 0, 0),
                    pipeline_mode=pl.Buffered(1),
                ),
            ],
            out_specs=pl.BlockSpec((1, tile, width), lambda t, c, n: (t, 0, 0)),
        ),
        compiler_params=pltpu.CompilerParams(vmem_limit_bytes=VMEM_LIMIT),
    )(cols, counts, tile_values, x_tiles)


def aggregate_transposed(tile_values, cols, counts, g_tiles, col_tiles):
    row_tiles, slots, tile, _ = tile_values.shape
    width = g_tiles.shape[-1]
    return pl.pallas_call(
        backward_kernel,
        out_shape=jax.ShapeDtypeStruct((col_tiles, tile, width), jnp.bfloat16),
        grid_spec=pltpu.PrefetchScalarGridSpec(
            num_scalar_prefetch=2,
            grid=(row_tiles,),
            in_specs=[
                pl.BlockSpec((1, slots, tile, tile), lambda t, c, n: (t, 0, 0, 0)),
                pl.BlockSpec((1, tile, width), lambda t, c, n: (t, 0, 0)),
            ],
            out_specs=pl.BlockSpec((col_tiles, tile, width), lambda t, c, n: (0, 0, 0)),
            scratch_shapes=[pltpu.VMEM((col_tiles, tile, width), jnp.float32)],
        ),
        compiler_params=pltpu.CompilerParams(vmem_limit_bytes=VMEM_LIMIT),
    )(cols, counts, tile_values, g_tiles)


def gather_over(x, axis):
    size = lax.axis_size(axis)
    spread = jnp.broadcast_to(x[None], (size,) + x.shape)
    got = lax.all_to_all(spread, axis, 0, 0, tiled=True)
    return got.reshape((size * x.shape[0],) + x.shape[1:])


def sum_scatter_over(x, axis):
    size = lax.axis_size(axis)
    parts = x.reshape((size, x.shape[0] // size) + x.shape[1:])
    got = lax.all_to_all(parts, axis, 0, 0, tiled=True)
    return got.astype(jnp.float32).sum(axis=0)


def dense_part(hidden, weight, bias, cotangent):
    preact = jnp.dot(hidden, weight, preferred_element_type=jnp.float32) + bias
    output = jax.nn.silu(preact).astype(jnp.bfloat16)
    sigmoid_value = jax.nn.sigmoid(preact)
    slope = sigmoid_value * (1.0 + preact * (1.0 - sigmoid_value))
    preact_grad = (cotangent.astype(jnp.float32) * slope).astype(jnp.bfloat16)
    weight_grad = lax.dot_general(
        hidden, preact_grad, (((0,), (0,)), ((), ())), preferred_element_type=jnp.float32
    )
    bias_grad = jnp.sum(preact_grad.astype(jnp.float32), axis=0)
    hidden_grad = lax.dot_general(
        preact_grad, weight, (((1,), (1,)), ((), ())), preferred_element_type=jnp.float32
    ).astype(jnp.bfloat16)
    return (output, weight_grad, bias_grad, hidden_grad)


def all_sum(weight_grad, bias_grad):
    axes = ("row", "col")
    devices = lax.axis_size("row") * lax.axis_size("col")
    width = weight_grad.shape[1]
    rows = weight_grad.shape[0] + 1
    per = -(-rows // devices)
    packed = jnp.concatenate(
        [weight_grad, bias_grad[None], jnp.zeros((per * devices - rows, width), jnp.float32)]
    )
    parts = lax.all_to_all(packed.reshape(devices, per, width), axes, 0, 0, tiled=True)
    summed = parts.sum(axis=0, keepdims=True)
    spread = jnp.broadcast_to(summed, (devices, per, width))
    back = lax.all_to_all(spread, axes, 0, 0, tiled=True).reshape(devices * per, width)
    return back[: rows - 1], back[rows - 1]


def per_device(features, tile_values, tile_cols, tile_counts, weight, bias, cotangent):
    node_dev, width = features.shape
    row_tiles, slot_count, tile_size, _ = tile_values.shape
    column_block = gather_over(features, "col")
    column_tiles = column_block.shape[0] // tile_size
    x_tiles = column_block.reshape(column_tiles, tile_size, width)
    live_counts = tile_counts[:, 0]

    partial_value = aggregate(tile_values, tile_cols, live_counts, x_tiles)
    partial_value = partial_value.reshape(row_tiles * tile_size, width)
    node_total = node_dev * lax.axis_size("row") * lax.axis_size("col")
    grad_scale = 1.0 / math.sqrt(node_total)
    own_rows = sum_scatter_over(partial_value, "row").astype(jnp.bfloat16)
    layer_out, weight_grad, bias_grad, hidden_grad = dense_part(own_rows, weight, bias, cotangent)
    weight_grad, bias_grad = all_sum(weight_grad, bias_grad)
    grad_block = gather_over(hidden_grad, "row")
    grad_tiles = grad_block.reshape(row_tiles, tile_size, width)

    summed = aggregate_transposed(tile_values, tile_cols, live_counts, grad_tiles, column_tiles)
    summed = summed.reshape(column_tiles * tile_size, width)
    feature_grad = sum_scatter_over(summed, "col").astype(jnp.bfloat16)
    return (layer_out, feature_grad, weight_grad * grad_scale, bias_grad * grad_scale)


def solution(mesh):
    placed = (
        P(("row", "col"), None),
        P("col", "row", None, None),
        P("col", "row"),
        P("col", "row"),
        P(),
        P(),
        P(("col", "row"), None),
    )
    return jax.shard_map(
        per_device,
        mesh=mesh,
        in_specs=placed,
        out_specs=(P(("col", "row"), None), P(("row", "col"), None), P(), P()),
        check_vma=False,
    )
```

```python
import functools
import math

import jax
import jax.numpy as jnp
from jax import lax
from jax.experimental import pallas as pl
from jax.experimental.pallas import tpu as pltpu
from jax.sharding import PartitionSpec as P

VMEM_LIMIT = 60 * 1024 * 1024


def forward_kernel(cols_ref, counts_ref, a_ref, x_ref, o_ref):
    t = pl.program_id(0)
    slots = a_ref.shape[1]
    last = x_ref.shape[0] - 1
    live = counts_ref[t]
    acc = None
    for s in range(slots):
        j = jnp.clip(cols_ref[t, s], 0, last)
        term = jnp.dot(a_ref[0, s], x_ref[j], preferred_element_type=jnp.float32)
        term = jnp.where(s < live, term, 0.0)
        acc = term if acc is None else acc + term
    o_ref[0] = acc.astype(o_ref.dtype)


def backward_kernel(cols_ref, counts_ref, a_ref, g_ref, o_ref, acc_ref):
    t = pl.program_id(0)
    slots = a_ref.shape[1]
    last = acc_ref.shape[0] - 1
    live = counts_ref[t]

    @pl.when(t == 0)
    def _():
        acc_ref[...] = jnp.zeros_like(acc_ref)

    g = g_ref[0]
    for s in range(slots):
        j = jnp.clip(cols_ref[t, s], 0, last)
        term = lax.dot_general(
            a_ref[0, s], g, (((0,), (0,)), ((), ())), preferred_element_type=jnp.float32
        )
        acc_ref[j] += jnp.where(s < live, term, 0.0)

    @pl.when(t == pl.num_programs(0) - 1)
    def _():
        def put(j, carry):
            o_ref[j] = acc_ref[j].astype(o_ref.dtype)
            return carry

        lax.fori_loop(0, acc_ref.shape[0], put, 0)


def aggregate(tile_values, cols, counts, x_tiles):
    row_tiles, slots, tile, _ = tile_values.shape
    col_tiles, _, width = x_tiles.shape
    return pl.pallas_call(
        forward_kernel,
        out_shape=jax.ShapeDtypeStruct((row_tiles, tile, width), jnp.bfloat16),
        grid_spec=pltpu.PrefetchScalarGridSpec(
            num_scalar_prefetch=2,
            grid=(row_tiles,),
            in_specs=[
                pl.BlockSpec((1, slots, tile, tile), lambda t, c, n: (t, 0, 0, 0)),
                pl.BlockSpec(
                    (col_tiles, tile, width),
                    lambda t, c, n: (0, 0, 0),
                    pipeline_mode=pl.Buffered(1),
                ),
            ],
            out_specs=pl.BlockSpec((1, tile, width), lambda t, c, n: (t, 0, 0)),
        ),
        compiler_params=pltpu.CompilerParams(vmem_limit_bytes=VMEM_LIMIT),
    )(cols, counts, tile_values, x_tiles)


def aggregate_transposed(tile_values, cols, counts, g_tiles, col_tiles):
    row_tiles, slots, tile, _ = tile_values.shape
    width = g_tiles.shape[-1]
    return pl.pallas_call(
        backward_kernel,
        out_shape=jax.ShapeDtypeStruct((col_tiles, tile, width), jnp.bfloat16),
        grid_spec=pltpu.PrefetchScalarGridSpec(
            num_scalar_prefetch=2,
            grid=(row_tiles,),
            in_specs=[
                pl.BlockSpec((1, slots, tile, tile), lambda t, c, n: (t, 0, 0, 0)),
                pl.BlockSpec((1, tile, width), lambda t, c, n: (t, 0, 0)),
            ],
            out_specs=pl.BlockSpec((col_tiles, tile, width), lambda t, c, n: (0, 0, 0)),
            scratch_shapes=[pltpu.VMEM((col_tiles, tile, width), jnp.float32)],
        ),
        compiler_params=pltpu.CompilerParams(vmem_limit_bytes=VMEM_LIMIT),
    )(cols, counts, tile_values, g_tiles)


def gather_over(x, axis):
    size = lax.axis_size(axis)
    spread = jnp.broadcast_to(x[None], (size,) + x.shape)
    got = lax.all_to_all(spread, axis, 0, 0, tiled=True)
    return got.reshape((size * x.shape[0],) + x.shape[1:])


def sum_scatter_over(x, axis):
    size = lax.axis_size(axis)
    parts = x.reshape((size, x.shape[0] // size) + x.shape[1:])
    got = lax.all_to_all(parts, axis, 0, 0, tiled=True)
    return got.astype(jnp.float32).sum(axis=0)


def dense_part(hidden, weight, bias, cotangent):
    preact = jnp.dot(hidden, weight, preferred_element_type=jnp.float32) + bias
    output = jax.nn.silu(preact).astype(jnp.bfloat16)
    sigmoid_value = jax.nn.sigmoid(preact)
    slope = sigmoid_value * (1.0 + preact * (1.0 - sigmoid_value))
    preact_grad = (cotangent.astype(jnp.float32) * slope).astype(jnp.bfloat16)
    weight_grad = lax.dot_general(
        hidden, preact_grad, (((0,), (0,)), ((), ())), preferred_element_type=jnp.float32
    )
    bias_grad = jnp.sum(preact_grad.astype(jnp.float32), axis=0)
    hidden_grad = lax.dot_general(
        preact_grad, weight, (((1,), (1,)), ((), ())), preferred_element_type=jnp.float32
    ).astype(jnp.bfloat16)
    return (output, weight_grad, bias_grad, hidden_grad)


def all_sum(weight_grad, bias_grad):
    axes = ("row", "col")
    devices = lax.axis_size("row") * lax.axis_size("col")
    width = weight_grad.shape[1]
    rows = weight_grad.shape[0] + 1
    per = -(-rows // devices)
    packed = jnp.concatenate(
        [weight_grad, bias_grad[None], jnp.zeros((per * devices - rows, width), jnp.float32)]
    )
    parts = lax.all_to_all(packed.reshape(devices, per, width), axes, 0, 0, tiled=True)
    summed = parts.sum(axis=0, keepdims=True)
    spread = jnp.broadcast_to(summed, (devices, per, width))
    back = lax.all_to_all(spread, axes, 0, 0, tiled=True).reshape(devices * per, width)
    return back[: rows - 1], back[rows - 1]


def per_device(features, tile_values, tile_cols, tile_counts, weight, bias, cotangent):
    node_dev, width = features.shape
    row_tiles, slot_count, tile_size, _ = tile_values.shape
    column_block = gather_over(features, "col")
    column_tiles = column_block.shape[0] // tile_size
    x_tiles = column_block.reshape(column_tiles, tile_size, width)
    live_counts = tile_counts[:, 0]

    partial_value = aggregate(tile_values, tile_cols, live_counts, x_tiles)
    partial_value = partial_value.reshape(row_tiles * tile_size, width)
    node_total = node_dev * lax.axis_size("row") * lax.axis_size("col")
    grad_scale = 1.0 / math.sqrt(node_total)
    own_rows = sum_scatter_over(partial_value, "row").astype(jnp.bfloat16)
    layer_out, weight_grad, bias_grad, hidden_grad = dense_part(own_rows, weight, bias, cotangent)
    weight_grad, bias_grad = all_sum(weight_grad, bias_grad)
    grad_block = gather_over(hidden_grad, "row")
    grad_block, weight_grad, bias_grad = lax.optimization_barrier((grad_block, weight_grad, bias_grad))
    grad_tiles = grad_block.reshape(row_tiles, tile_size, width)

    summed = aggregate_transposed(tile_values, tile_cols, live_counts, grad_tiles, column_tiles)
    summed = summed.reshape(column_tiles * tile_size, width)
    feature_grad = sum_scatter_over(summed, "col").astype(jnp.bfloat16)
    return (layer_out, feature_grad, weight_grad * grad_scale, bias_grad * grad_scale)


def solution(mesh):
    placed = (
        P(("row", "col"), None),
        P("col", "row", None, None),
        P("col", "row"),
        P("col", "row"),
        P(),
        P(),
        P(("col", "row"), None),
    )
    return jax.shard_map(
        per_device,
        mesh=mesh,
        in_specs=placed,
        out_specs=(P(("col", "row"), None), P(("row", "col"), None), P(), P()),
        check_vma=False,
    )
```

```python
import functools
import math

import jax
import jax.numpy as jnp
from jax import lax
from jax.experimental import pallas as pl
from jax.experimental.pallas import tpu as pltpu
from jax.sharding import PartitionSpec as P

VMEM_LIMIT = 60 * 1024 * 1024


def forward_kernel(cols_ref, counts_ref, a_ref, x_ref, o_ref):
    t = pl.program_id(0)
    slots = a_ref.shape[1]
    last = x_ref.shape[0] - 1
    live = counts_ref[t]
    acc = None
    for s in range(slots):
        j = jnp.clip(cols_ref[t, s], 0, last)
        term = jnp.dot(a_ref[0, s], x_ref[j], preferred_element_type=jnp.float32)
        term = jnp.where(s < live, term, 0.0)
        acc = term if acc is None else acc + term
    o_ref[0] = acc.astype(o_ref.dtype)


def backward_kernel(cols_ref, counts_ref, a_ref, g_ref, o_ref, acc_ref):
    t = pl.program_id(0)
    slots = a_ref.shape[1]
    last = acc_ref.shape[0] - 1
    live = counts_ref[t]

    @pl.when(t == 0)
    def _():
        acc_ref[...] = jnp.zeros_like(acc_ref)

    g = g_ref[0]
    for s in range(slots):
        j = jnp.clip(cols_ref[t, s], 0, last)
        term = lax.dot_general(
            a_ref[0, s], g, (((0,), (0,)), ((), ())), preferred_element_type=jnp.float32
        )
        acc_ref[j] += jnp.where(s < live, term, 0.0)

    @pl.when(t == pl.num_programs(0) - 1)
    def _():
        def put(j, carry):
            o_ref[j] = acc_ref[j].astype(o_ref.dtype)
            return carry

        lax.fori_loop(0, acc_ref.shape[0], put, 0)


def aggregate(tile_values, cols, counts, x_tiles):
    row_tiles, slots, tile, _ = tile_values.shape
    col_tiles, _, width = x_tiles.shape
    return pl.pallas_call(
        forward_kernel,
        out_shape=jax.ShapeDtypeStruct((row_tiles, tile, width), jnp.bfloat16),
        grid_spec=pltpu.PrefetchScalarGridSpec(
            num_scalar_prefetch=2,
            grid=(row_tiles,),
            in_specs=[
                pl.BlockSpec((1, slots, tile, tile), lambda t, c, n: (t, 0, 0, 0)),
                pl.BlockSpec(
                    (col_tiles, tile, width),
                    lambda t, c, n: (0, 0, 0),
                    pipeline_mode=pl.Buffered(1),
                ),
            ],
            out_specs=pl.BlockSpec((1, tile, width), lambda t, c, n: (t, 0, 0)),
        ),
        compiler_params=pltpu.CompilerParams(vmem_limit_bytes=VMEM_LIMIT),
    )(cols, counts, tile_values, x_tiles)


def aggregate_transposed(tile_values, cols, counts, g_tiles, col_tiles):
    row_tiles, slots, tile, _ = tile_values.shape
    width = g_tiles.shape[-1]
    return pl.pallas_call(
        backward_kernel,
        out_shape=jax.ShapeDtypeStruct((col_tiles, tile, width), jnp.bfloat16),
        grid_spec=pltpu.PrefetchScalarGridSpec(
            num_scalar_prefetch=2,
            grid=(row_tiles,),
            in_specs=[
                pl.BlockSpec((1, slots, tile, tile), lambda t, c, n: (t, 0, 0, 0)),
                pl.BlockSpec((1, tile, width), lambda t, c, n: (t, 0, 0)),
            ],
            out_specs=pl.BlockSpec((col_tiles, tile, width), lambda t, c, n: (0, 0, 0)),
            scratch_shapes=[pltpu.VMEM((col_tiles, tile, width), jnp.float32)],
        ),
        compiler_params=pltpu.CompilerParams(vmem_limit_bytes=VMEM_LIMIT),
    )(cols, counts, tile_values, g_tiles)


def gather_over(x, axis):
    size = lax.axis_size(axis)
    spread = jnp.broadcast_to(x[None], (size,) + x.shape)
    got = lax.all_to_all(spread, axis, 0, 0, tiled=True)
    return got.reshape((size * x.shape[0],) + x.shape[1:])


def sum_scatter_over(x, axis):
    size = lax.axis_size(axis)
    parts = x.reshape((size, x.shape[0] // size) + x.shape[1:])
    got = lax.all_to_all(parts, axis, 0, 0, tiled=True)
    return got.astype(jnp.float32).sum(axis=0)


def dense_part(hidden, weight, bias, cotangent):
    preact = jnp.dot(hidden, weight, preferred_element_type=jnp.float32) + bias
    output = jax.nn.silu(preact).astype(jnp.bfloat16)
    sigmoid_value = jax.nn.sigmoid(preact)
    slope = sigmoid_value * (1.0 + preact * (1.0 - sigmoid_value))
    preact_grad = (cotangent.astype(jnp.float32) * slope).astype(jnp.bfloat16)
    weight_grad = lax.dot_general(
        hidden, preact_grad, (((0,), (0,)), ((), ())), preferred_element_type=jnp.float32
    )
    bias_grad = jnp.sum(preact_grad.astype(jnp.float32), axis=0)
    hidden_grad = lax.dot_general(
        preact_grad, weight, (((1,), (1,)), ((), ())), preferred_element_type=jnp.float32
    ).astype(jnp.bfloat16)
    return (output, weight_grad, bias_grad, hidden_grad)


def all_sum(weight_grad, bias_grad):
    axes = ("row", "col")
    devices = lax.axis_size("row") * lax.axis_size("col")
    width = weight_grad.shape[1]
    rows = weight_grad.shape[0] + 1
    per = -(-rows // devices)
    packed = jnp.concatenate(
        [weight_grad, bias_grad[None], jnp.zeros((per * devices - rows, width), jnp.float32)]
    )
    parts = lax.all_to_all(packed.reshape(devices, per, width), axes, 0, 0, tiled=True)
    summed = parts.sum(axis=0, keepdims=True)
    spread = jnp.broadcast_to(summed, (devices, per, width))
    back = lax.all_to_all(spread, axes, 0, 0, tiled=True).reshape(devices * per, width)
    return back[: rows - 1], back[rows - 1]


def per_device(features, tile_values, tile_cols, tile_counts, weight, bias, cotangent):
    node_dev, width = features.shape
    row_tiles, slot_count, tile_size, _ = tile_values.shape
    column_block = gather_over(features, "col")
    column_tiles = column_block.shape[0] // tile_size
    x_tiles = column_block.reshape(column_tiles, tile_size, width)
    live_counts = tile_counts[:, 0]

    partial_value = aggregate(tile_values, tile_cols, live_counts, x_tiles)
    partial_value = partial_value.reshape(row_tiles * tile_size, width)
    node_total = node_dev * lax.axis_size("row") * lax.axis_size("col")
    grad_scale = 1.0 / math.sqrt(node_total)
    own_rows = sum_scatter_over(partial_value, "row").astype(jnp.bfloat16)
    layer_out, weight_grad, bias_grad, hidden_grad = dense_part(own_rows, weight, bias, cotangent)
    weight_grad, bias_grad = all_sum(weight_grad * grad_scale, bias_grad * grad_scale)
    grad_block = gather_over(hidden_grad, "row")
    grad_tiles = grad_block.reshape(row_tiles, tile_size, width)

    summed = aggregate_transposed(tile_values, tile_cols, live_counts, grad_tiles, column_tiles)
    summed = summed.reshape(column_tiles * tile_size, width)
    feature_grad = sum_scatter_over(summed, "col").astype(jnp.bfloat16)
    return (layer_out, feature_grad, weight_grad, bias_grad)


def solution(mesh):
    placed = (
        P(("row", "col"), None),
        P("col", "row", None, None),
        P("col", "row"),
        P("col", "row"),
        P(),
        P(),
        P(("col", "row"), None),
    )
    return jax.shard_map(
        per_device,
        mesh=mesh,
        in_specs=placed,
        out_specs=(P(("col", "row"), None), P(("row", "col"), None), P(), P()),
        check_vma=False,
    )
```

```python
import functools
import math

import jax
import jax.numpy as jnp
from jax import lax
from jax.experimental import pallas as pl
from jax.experimental.pallas import tpu as pltpu
from jax.sharding import PartitionSpec as P

VMEM_LIMIT = 60 * 1024 * 1024


def forward_kernel(cols_ref, counts_ref, a_ref, x_ref, o_ref, acc_ref):
    t = pl.program_id(0)
    slots = a_ref.shape[1]
    last = x_ref.shape[0] - 1
    live = counts_ref[t]
    j = jnp.clip(cols_ref[t, 0], 0, last)
    first = jnp.dot(a_ref[0, 0], x_ref[j], preferred_element_type=jnp.float32)
    acc_ref[...] = jnp.where(live > 0, first, 0.0)
    for s in range(1, slots):

        @pl.when(s < live)
        def _():
            k = jnp.clip(cols_ref[t, s], 0, last)
            acc_ref[...] += jnp.dot(a_ref[0, s], x_ref[k], preferred_element_type=jnp.float32)

    o_ref[0] = acc_ref[...].astype(o_ref.dtype)


def backward_kernel(cols_ref, counts_ref, a_ref, g_ref, o_ref, acc_ref):
    t = pl.program_id(0)
    slots = a_ref.shape[1]
    last = acc_ref.shape[0] - 1
    live = counts_ref[t]

    @pl.when(t == 0)
    def _():
        acc_ref[...] = jnp.zeros_like(acc_ref)

    g = g_ref[0]
    for s in range(slots):

        @pl.when(s < live)
        def _():
            j = jnp.clip(cols_ref[t, s], 0, last)
            acc_ref[j] += lax.dot_general(
                a_ref[0, s], g, (((0,), (0,)), ((), ())), preferred_element_type=jnp.float32
            )

    @pl.when(t == pl.num_programs(0) - 1)
    def _():
        def put(j, carry):
            o_ref[j] = acc_ref[j].astype(o_ref.dtype)
            return carry

        lax.fori_loop(0, acc_ref.shape[0], put, 0)


def aggregate(tile_values, cols, counts, x_tiles):
    row_tiles, slots, tile, _ = tile_values.shape
    col_tiles, _, width = x_tiles.shape
    return pl.pallas_call(
        forward_kernel,
        out_shape=jax.ShapeDtypeStruct((row_tiles, tile, width), jnp.bfloat16),
        grid_spec=pltpu.PrefetchScalarGridSpec(
            num_scalar_prefetch=2,
            grid=(row_tiles,),
            in_specs=[
                pl.BlockSpec((1, slots, tile, tile), lambda t, c, n: (t, 0, 0, 0)),
                pl.BlockSpec(
                    (col_tiles, tile, width),
                    lambda t, c, n: (0, 0, 0),
                    pipeline_mode=pl.Buffered(1),
                ),
            ],
            out_specs=pl.BlockSpec((1, tile, width), lambda t, c, n: (t, 0, 0)),
            scratch_shapes=[pltpu.VMEM((tile, width), jnp.float32)],
        ),
        compiler_params=pltpu.CompilerParams(vmem_limit_bytes=VMEM_LIMIT),
    )(cols, counts, tile_values, x_tiles)


def aggregate_transposed(tile_values, cols, counts, g_tiles, col_tiles):
    row_tiles, slots, tile, _ = tile_values.shape
    width = g_tiles.shape[-1]
    return pl.pallas_call(
        backward_kernel,
        out_shape=jax.ShapeDtypeStruct((col_tiles, tile, width), jnp.bfloat16),
        grid_spec=pltpu.PrefetchScalarGridSpec(
            num_scalar_prefetch=2,
            grid=(row_tiles,),
            in_specs=[
                pl.BlockSpec((1, slots, tile, tile), lambda t, c, n: (t, 0, 0, 0)),
                pl.BlockSpec((1, tile, width), lambda t, c, n: (t, 0, 0)),
            ],
            out_specs=pl.BlockSpec((col_tiles, tile, width), lambda t, c, n: (0, 0, 0)),
            scratch_shapes=[pltpu.VMEM((col_tiles, tile, width), jnp.float32)],
        ),
        compiler_params=pltpu.CompilerParams(vmem_limit_bytes=VMEM_LIMIT),
    )(cols, counts, tile_values, g_tiles)


def gather_over(x, axis):
    size = lax.axis_size(axis)
    spread = jnp.broadcast_to(x[None], (size,) + x.shape)
    got = lax.all_to_all(spread, axis, 0, 0, tiled=True)
    return got.reshape((size * x.shape[0],) + x.shape[1:])


def sum_scatter_over(x, axis):
    size = lax.axis_size(axis)
    parts = x.reshape((size, x.shape[0] // size) + x.shape[1:])
    got = lax.all_to_all(parts, axis, 0, 0, tiled=True)
    return got.astype(jnp.float32).sum(axis=0)


def dense_part(hidden, weight, bias, cotangent):
    preact = jnp.dot(hidden, weight, preferred_element_type=jnp.float32) + bias
    output = jax.nn.silu(preact).astype(jnp.bfloat16)
    sigmoid_value = jax.nn.sigmoid(preact)
    slope = sigmoid_value * (1.0 + preact * (1.0 - sigmoid_value))
    preact_grad = (cotangent.astype(jnp.float32) * slope).astype(jnp.bfloat16)
    weight_grad = lax.dot_general(
        hidden, preact_grad, (((0,), (0,)), ((), ())), preferred_element_type=jnp.float32
    )
    bias_grad = jnp.sum(preact_grad.astype(jnp.float32), axis=0)
    hidden_grad = lax.dot_general(
        preact_grad, weight, (((1,), (1,)), ((), ())), preferred_element_type=jnp.float32
    ).astype(jnp.bfloat16)
    return (output, weight_grad, bias_grad, hidden_grad)


def all_sum(weight_grad, bias_grad):
    axes = ("row", "col")
    devices = lax.axis_size("row") * lax.axis_size("col")
    width = weight_grad.shape[1]
    rows = weight_grad.shape[0] + 1
    per = -(-rows // devices)
    packed = jnp.concatenate(
        [weight_grad, bias_grad[None], jnp.zeros((per * devices - rows, width), jnp.float32)]
    )
    parts = lax.all_to_all(packed.reshape(devices, per, width), axes, 0, 0, tiled=True)
    summed = parts.sum(axis=0, keepdims=True)
    spread = jnp.broadcast_to(summed, (devices, per, width))
    back = lax.all_to_all(spread, axes, 0, 0, tiled=True).reshape(devices * per, width)
    return back[: rows - 1], back[rows - 1]


def per_device(features, tile_values, tile_cols, tile_counts, weight, bias, cotangent):
    node_dev, width = features.shape
    row_tiles, slot_count, tile_size, _ = tile_values.shape
    column_block = gather_over(features, "col")
    column_tiles = column_block.shape[0] // tile_size
    x_tiles = column_block.reshape(column_tiles, tile_size, width)
    live_counts = tile_counts[:, 0]

    partial_value = aggregate(tile_values, tile_cols, live_counts, x_tiles)
    partial_value = partial_value.reshape(row_tiles * tile_size, width)
    node_total = node_dev * lax.axis_size("row") * lax.axis_size("col")
    grad_scale = 1.0 / math.sqrt(node_total)
    own_rows = sum_scatter_over(partial_value, "row").astype(jnp.bfloat16)
    layer_out, weight_grad, bias_grad, hidden_grad = dense_part(own_rows, weight, bias, cotangent)
    weight_grad, bias_grad = all_sum(weight_grad * grad_scale, bias_grad * grad_scale)
    grad_block = gather_over(hidden_grad, "row")
    grad_tiles = grad_block.reshape(row_tiles, tile_size, width)

    summed = aggregate_transposed(tile_values, tile_cols, live_counts, grad_tiles, column_tiles)
    summed = summed.reshape(column_tiles * tile_size, width)
    feature_grad = sum_scatter_over(summed, "col").astype(jnp.bfloat16)
    return (layer_out, feature_grad, weight_grad, bias_grad)


def solution(mesh):
    placed = (
        P(("row", "col"), None),
        P("col", "row", None, None),
        P("col", "row"),
        P("col", "row"),
        P(),
        P(),
        P(("col", "row"), None),
    )
    return jax.shard_map(
        per_device,
        mesh=mesh,
        in_specs=placed,
        out_specs=(P(("col", "row"), None), P(("row", "col"), None), P(), P()),
        check_vma=False,
    )
```

```python
import functools
import math

import jax
import jax.numpy as jnp
from jax import lax
from jax.experimental import pallas as pl
from jax.experimental.pallas import tpu as pltpu
from jax.sharding import PartitionSpec as P

VMEM_LIMIT = 60 * 1024 * 1024
GROUP = 2


def forward_kernel(cols_ref, counts_ref, a_ref, x_ref, o_ref):
    step = pl.program_id(0)
    group, slots = a_ref.shape[:2]
    last = x_ref.shape[0] - 1
    for u in range(group):
        t = step * group + u
        live = counts_ref[t]
        acc = None
        for s in range(slots):
            j = jnp.clip(cols_ref[t, s], 0, last)
            term = jnp.dot(a_ref[u, s], x_ref[j], preferred_element_type=jnp.float32)
            term = jnp.where(s < live, term, 0.0)
            acc = term if acc is None else acc + term
        o_ref[u] = acc.astype(o_ref.dtype)


def backward_kernel(cols_ref, counts_ref, a_ref, g_ref, o_ref, acc_ref):
    step = pl.program_id(0)
    group, slots = a_ref.shape[:2]
    last = acc_ref.shape[0] - 1

    @pl.when(step == 0)
    def _():
        acc_ref[...] = jnp.zeros_like(acc_ref)

    for u in range(group):
        t = step * group + u
        live = counts_ref[t]
        g = g_ref[u]
        terms = [
            lax.dot_general(
                a_ref[u, s], g, (((0,), (0,)), ((), ())), preferred_element_type=jnp.float32
            )
            for s in range(slots)
        ]
        for s in range(slots):
            j = jnp.clip(cols_ref[t, s], 0, last)
            acc_ref[j] += jnp.where(s < live, terms[s], 0.0)

    @pl.when(step == pl.num_programs(0) - 1)
    def _():
        def put(j, carry):
            o_ref[j] = acc_ref[j].astype(o_ref.dtype)
            return carry

        lax.fori_loop(0, acc_ref.shape[0], put, 0)


def aggregate(tile_values, cols, counts, x_tiles):
    row_tiles, slots, tile, _ = tile_values.shape
    col_tiles, _, width = x_tiles.shape
    return pl.pallas_call(
        forward_kernel,
        out_shape=jax.ShapeDtypeStruct((row_tiles, tile, width), jnp.bfloat16),
        grid_spec=pltpu.PrefetchScalarGridSpec(
            num_scalar_prefetch=2,
            grid=(row_tiles // GROUP,),
            in_specs=[
                pl.BlockSpec((GROUP, slots, tile, tile), lambda t, c, n: (t, 0, 0, 0)),
                pl.BlockSpec(
                    (col_tiles, tile, width),
                    lambda t, c, n: (0, 0, 0),
                    pipeline_mode=pl.Buffered(1),
                ),
            ],
            out_specs=pl.BlockSpec((GROUP, tile, width), lambda t, c, n: (t, 0, 0)),
        ),
        compiler_params=pltpu.CompilerParams(vmem_limit_bytes=VMEM_LIMIT),
    )(cols, counts, tile_values, x_tiles)


def aggregate_transposed(tile_values, cols, counts, g_tiles, col_tiles):
    row_tiles, slots, tile, _ = tile_values.shape
    width = g_tiles.shape[-1]
    return pl.pallas_call(
        backward_kernel,
        out_shape=jax.ShapeDtypeStruct((col_tiles, tile, width), jnp.bfloat16),
        grid_spec=pltpu.PrefetchScalarGridSpec(
            num_scalar_prefetch=2,
            grid=(row_tiles // GROUP,),
            in_specs=[
                pl.BlockSpec((GROUP, slots, tile, tile), lambda t, c, n: (t, 0, 0, 0)),
                pl.BlockSpec((GROUP, tile, width), lambda t, c, n: (t, 0, 0)),
            ],
            out_specs=pl.BlockSpec((col_tiles, tile, width), lambda t, c, n: (0, 0, 0)),
            scratch_shapes=[pltpu.VMEM((col_tiles, tile, width), jnp.float32)],
        ),
        compiler_params=pltpu.CompilerParams(vmem_limit_bytes=VMEM_LIMIT),
    )(cols, counts, tile_values, g_tiles)


def gather_over(x, axis):
    size = lax.axis_size(axis)
    spread = jnp.broadcast_to(x[None], (size,) + x.shape)
    got = lax.all_to_all(spread, axis, 0, 0, tiled=True)
    return got.reshape((size * x.shape[0],) + x.shape[1:])


def sum_scatter_over(x, axis):
    size = lax.axis_size(axis)
    parts = x.reshape((size, x.shape[0] // size) + x.shape[1:])
    got = lax.all_to_all(parts, axis, 0, 0, tiled=True)
    return got.astype(jnp.float32).sum(axis=0)


def dense_part(hidden, weight, bias, cotangent):
    preact = jnp.dot(hidden, weight, preferred_element_type=jnp.float32) + bias
    output = jax.nn.silu(preact).astype(jnp.bfloat16)
    sigmoid_value = jax.nn.sigmoid(preact)
    slope = sigmoid_value * (1.0 + preact * (1.0 - sigmoid_value))
    preact_grad = (cotangent.astype(jnp.float32) * slope).astype(jnp.bfloat16)
    weight_grad = lax.dot_general(
        hidden, preact_grad, (((0,), (0,)), ((), ())), preferred_element_type=jnp.float32
    )
    bias_grad = jnp.sum(preact_grad.astype(jnp.float32), axis=0)
    hidden_grad = lax.dot_general(
        preact_grad, weight, (((1,), (1,)), ((), ())), preferred_element_type=jnp.float32
    ).astype(jnp.bfloat16)
    return (output, weight_grad, bias_grad, hidden_grad)


def all_sum(weight_grad, bias_grad):
    axes = ("row", "col")
    devices = lax.axis_size("row") * lax.axis_size("col")
    width = weight_grad.shape[1]
    rows = weight_grad.shape[0] + 1
    per = -(-rows // devices)
    packed = jnp.concatenate(
        [weight_grad, bias_grad[None], jnp.zeros((per * devices - rows, width), jnp.float32)]
    )
    parts = lax.all_to_all(packed.reshape(devices, per, width), axes, 0, 0, tiled=True)
    summed = parts.sum(axis=0, keepdims=True)
    spread = jnp.broadcast_to(summed, (devices, per, width))
    back = lax.all_to_all(spread, axes, 0, 0, tiled=True).reshape(devices * per, width)
    return back[: rows - 1], back[rows - 1]


def per_device(features, tile_values, tile_cols, tile_counts, weight, bias, cotangent):
    node_dev, width = features.shape
    row_tiles, slot_count, tile_size, _ = tile_values.shape
    column_block = gather_over(features, "col")
    column_tiles = column_block.shape[0] // tile_size
    x_tiles = column_block.reshape(column_tiles, tile_size, width)
    live_counts = tile_counts[:, 0]

    partial_value = aggregate(tile_values, tile_cols, live_counts, x_tiles)
    partial_value = partial_value.reshape(row_tiles * tile_size, width)
    node_total = node_dev * lax.axis_size("row") * lax.axis_size("col")
    grad_scale = 1.0 / math.sqrt(node_total)
    own_rows = sum_scatter_over(partial_value, "row").astype(jnp.bfloat16)
    layer_out, weight_grad, bias_grad, hidden_grad = dense_part(own_rows, weight, bias, cotangent)
    weight_grad, bias_grad = all_sum(weight_grad * grad_scale, bias_grad * grad_scale)
    grad_block = gather_over(hidden_grad, "row")
    grad_tiles = grad_block.reshape(row_tiles, tile_size, width)

    summed = aggregate_transposed(tile_values, tile_cols, live_counts, grad_tiles, column_tiles)
    summed = summed.reshape(column_tiles * tile_size, width)
    feature_grad = sum_scatter_over(summed, "col").astype(jnp.bfloat16)
    return (layer_out, feature_grad, weight_grad, bias_grad)


def solution(mesh):
    placed = (
        P(("row", "col"), None),
        P("col", "row", None, None),
        P("col", "row"),
        P("col", "row"),
        P(),
        P(),
        P(("col", "row"), None),
    )
    return jax.shard_map(
        per_device,
        mesh=mesh,
        in_specs=placed,
        out_specs=(P(("col", "row"), None), P(("row", "col"), None), P(), P()),
        check_vma=False,
    )
```

```python
import functools
import math

import jax
import jax.numpy as jnp
from jax import lax
from jax.experimental import pallas as pl
from jax.experimental.pallas import tpu as pltpu
from jax.sharding import PartitionSpec as P

VMEM_LIMIT = 60 * 1024 * 1024
GROUP = 4


def forward_kernel(cols_ref, counts_ref, a_ref, x_ref, o_ref):
    step = pl.program_id(0)
    group, slots = a_ref.shape[:2]
    last = x_ref.shape[0] - 1
    for u in range(group):
        t = step * group + u
        live = counts_ref[t]
        acc = None
        for s in range(slots):
            j = jnp.clip(cols_ref[t, s], 0, last)
            term = jnp.dot(a_ref[u, s], x_ref[j], preferred_element_type=jnp.float32)
            term = jnp.where(s < live, term, 0.0)
            acc = term if acc is None else acc + term
        o_ref[u] = acc.astype(o_ref.dtype)


def backward_kernel(cols_ref, counts_ref, a_ref, g_ref, o_ref, acc_ref):
    step = pl.program_id(0)
    group, slots = a_ref.shape[:2]
    last = acc_ref.shape[0] - 1

    @pl.when(step == 0)
    def _():
        acc_ref[...] = jnp.zeros_like(acc_ref)

    for u in range(group):
        t = step * group + u
        live = counts_ref[t]
        g = g_ref[u]
        terms = [
            lax.dot_general(
                a_ref[u, s], g, (((0,), (0,)), ((), ())), preferred_element_type=jnp.float32
            )
            for s in range(slots)
        ]
        for s in range(slots):
            j = jnp.clip(cols_ref[t, s], 0, last)
            acc_ref[j] += jnp.where(s < live, terms[s], 0.0)

    @pl.when(step == pl.num_programs(0) - 1)
    def _():
        def put(j, carry):
            o_ref[j] = acc_ref[j].astype(o_ref.dtype)
            return carry

        lax.fori_loop(0, acc_ref.shape[0], put, 0)


def aggregate(tile_values, cols, counts, x_tiles):
    row_tiles, slots, tile, _ = tile_values.shape
    col_tiles, _, width = x_tiles.shape
    return pl.pallas_call(
        forward_kernel,
        out_shape=jax.ShapeDtypeStruct((row_tiles, tile, width), jnp.bfloat16),
        grid_spec=pltpu.PrefetchScalarGridSpec(
            num_scalar_prefetch=2,
            grid=(row_tiles // GROUP,),
            in_specs=[
                pl.BlockSpec((GROUP, slots, tile, tile), lambda t, c, n: (t, 0, 0, 0)),
                pl.BlockSpec(
                    (col_tiles, tile, width),
                    lambda t, c, n: (0, 0, 0),
                    pipeline_mode=pl.Buffered(1),
                ),
            ],
            out_specs=pl.BlockSpec((GROUP, tile, width), lambda t, c, n: (t, 0, 0)),
        ),
        compiler_params=pltpu.CompilerParams(vmem_limit_bytes=VMEM_LIMIT),
    )(cols, counts, tile_values, x_tiles)


def aggregate_transposed(tile_values, cols, counts, g_tiles, col_tiles):
    row_tiles, slots, tile, _ = tile_values.shape
    width = g_tiles.shape[-1]
    return pl.pallas_call(
        backward_kernel,
        out_shape=jax.ShapeDtypeStruct((col_tiles, tile, width), jnp.bfloat16),
        grid_spec=pltpu.PrefetchScalarGridSpec(
            num_scalar_prefetch=2,
            grid=(row_tiles // GROUP,),
            in_specs=[
                pl.BlockSpec((GROUP, slots, tile, tile), lambda t, c, n: (t, 0, 0, 0)),
                pl.BlockSpec((GROUP, tile, width), lambda t, c, n: (t, 0, 0)),
            ],
            out_specs=pl.BlockSpec((col_tiles, tile, width), lambda t, c, n: (0, 0, 0)),
            scratch_shapes=[pltpu.VMEM((col_tiles, tile, width), jnp.float32)],
        ),
        compiler_params=pltpu.CompilerParams(vmem_limit_bytes=VMEM_LIMIT),
    )(cols, counts, tile_values, g_tiles)


def gather_over(x, axis):
    size = lax.axis_size(axis)
    spread = jnp.broadcast_to(x[None], (size,) + x.shape)
    got = lax.all_to_all(spread, axis, 0, 0, tiled=True)
    return got.reshape((size * x.shape[0],) + x.shape[1:])


def sum_scatter_over(x, axis):
    size = lax.axis_size(axis)
    parts = x.reshape((size, x.shape[0] // size) + x.shape[1:])
    got = lax.all_to_all(parts, axis, 0, 0, tiled=True)
    return got.astype(jnp.float32).sum(axis=0)


def dense_part(hidden, weight, bias, cotangent):
    preact = jnp.dot(hidden, weight, preferred_element_type=jnp.float32) + bias
    output = jax.nn.silu(preact).astype(jnp.bfloat16)
    sigmoid_value = jax.nn.sigmoid(preact)
    slope = sigmoid_value * (1.0 + preact * (1.0 - sigmoid_value))
    preact_grad = (cotangent.astype(jnp.float32) * slope).astype(jnp.bfloat16)
    weight_grad = lax.dot_general(
        hidden, preact_grad, (((0,), (0,)), ((), ())), preferred_element_type=jnp.float32
    )
    bias_grad = jnp.sum(preact_grad.astype(jnp.float32), axis=0)
    hidden_grad = lax.dot_general(
        preact_grad, weight, (((1,), (1,)), ((), ())), preferred_element_type=jnp.float32
    ).astype(jnp.bfloat16)
    return (output, weight_grad, bias_grad, hidden_grad)


def all_sum(weight_grad, bias_grad):
    axes = ("row", "col")
    devices = lax.axis_size("row") * lax.axis_size("col")
    width = weight_grad.shape[1]
    rows = weight_grad.shape[0] + 1
    per = -(-rows // devices)
    packed = jnp.concatenate(
        [weight_grad, bias_grad[None], jnp.zeros((per * devices - rows, width), jnp.float32)]
    )
    parts = lax.all_to_all(packed.reshape(devices, per, width), axes, 0, 0, tiled=True)
    summed = parts.sum(axis=0, keepdims=True)
    spread = jnp.broadcast_to(summed, (devices, per, width))
    back = lax.all_to_all(spread, axes, 0, 0, tiled=True).reshape(devices * per, width)
    return back[: rows - 1], back[rows - 1]


def per_device(features, tile_values, tile_cols, tile_counts, weight, bias, cotangent):
    node_dev, width = features.shape
    row_tiles, slot_count, tile_size, _ = tile_values.shape
    column_block = gather_over(features, "col")
    column_tiles = column_block.shape[0] // tile_size
    x_tiles = column_block.reshape(column_tiles, tile_size, width)
    live_counts = tile_counts[:, 0]

    partial_value = aggregate(tile_values, tile_cols, live_counts, x_tiles)
    partial_value = partial_value.reshape(row_tiles * tile_size, width)
    node_total = node_dev * lax.axis_size("row") * lax.axis_size("col")
    grad_scale = 1.0 / math.sqrt(node_total)
    own_rows = sum_scatter_over(partial_value, "row").astype(jnp.bfloat16)
    layer_out, weight_grad, bias_grad, hidden_grad = dense_part(own_rows, weight, bias, cotangent)
    weight_grad, bias_grad = all_sum(weight_grad * grad_scale, bias_grad * grad_scale)
    grad_block = gather_over(hidden_grad, "row")
    grad_tiles = grad_block.reshape(row_tiles, tile_size, width)

    summed = aggregate_transposed(tile_values, tile_cols, live_counts, grad_tiles, column_tiles)
    summed = summed.reshape(column_tiles * tile_size, width)
    feature_grad = sum_scatter_over(summed, "col").astype(jnp.bfloat16)
    return (layer_out, feature_grad, weight_grad, bias_grad)


def solution(mesh):
    placed = (
        P(("row", "col"), None),
        P("col", "row", None, None),
        P("col", "row"),
        P("col", "row"),
        P(),
        P(),
        P(("col", "row"), None),
    )
    return jax.shard_map(
        per_device,
        mesh=mesh,
        in_specs=placed,
        out_specs=(P(("col", "row"), None), P(("row", "col"), None), P(), P()),
        check_vma=False,
    )
```

```python
import functools
import math

import jax
import jax.numpy as jnp
from jax import lax
from jax.experimental import pallas as pl
from jax.experimental.pallas import tpu as pltpu
from jax.sharding import PartitionSpec as P

VMEM_LIMIT = 60 * 1024 * 1024
GROUP = 4


def forward_kernel(cols_ref, counts_ref, a_ref, x_ref, o_ref):
    step = pl.program_id(0)
    group, slots = a_ref.shape[:2]
    last = x_ref.shape[0] - 1
    for u in range(group):
        t = step * group + u
        live = counts_ref[t]
        acc = None
        for s in range(slots):
            j = jnp.clip(cols_ref[t, s], 0, last)
            term = jnp.dot(a_ref[u, s], x_ref[j], preferred_element_type=jnp.float32)
            term = jnp.where(s < live, term, 0.0)
            acc = term if acc is None else acc + term
        o_ref[u] = acc.astype(o_ref.dtype)


def backward_kernel(cols_ref, counts_ref, a_ref, g_ref, o_ref, acc_ref):
    step = pl.program_id(0)
    group, slots = a_ref.shape[:2]
    last = acc_ref.shape[0] - 1

    @pl.when(step == 0)
    def _():
        acc_ref[...] = jnp.zeros_like(acc_ref)

    for u in range(group):
        t = step * group + u
        live = counts_ref[t]
        g = g_ref[u]
        terms = [
            lax.dot_general(
                a_ref[u, s], g, (((0,), (0,)), ((), ())), preferred_element_type=jnp.float32
            )
            for s in range(slots)
        ]
        for s in range(slots):
            j = jnp.clip(cols_ref[t, s], 0, last)
            acc_ref[j] += jnp.where(s < live, terms[s], 0.0)

    @pl.when(step == pl.num_programs(0) - 1)
    def _():
        def put(j, carry):
            o_ref[j] = acc_ref[j].astype(o_ref.dtype)
            return carry

        lax.fori_loop(0, acc_ref.shape[0], put, 0)


def aggregate(tile_values, cols, counts, x_tiles):
    row_tiles, slots, tile, _ = tile_values.shape
    col_tiles, _, width = x_tiles.shape
    return pl.pallas_call(
        forward_kernel,
        out_shape=jax.ShapeDtypeStruct((row_tiles, tile, width), jnp.bfloat16),
        grid_spec=pltpu.PrefetchScalarGridSpec(
            num_scalar_prefetch=2,
            grid=(row_tiles // GROUP,),
            in_specs=[
                pl.BlockSpec((GROUP, slots, tile, tile), lambda t, c, n: (t, 0, 0, 0)),
                pl.BlockSpec(
                    (col_tiles, tile, width),
                    lambda t, c, n: (0, 0, 0),
                    pipeline_mode=pl.Buffered(1),
                ),
            ],
            out_specs=pl.BlockSpec((GROUP, tile, width), lambda t, c, n: (t, 0, 0)),
        ),
        compiler_params=pltpu.CompilerParams(vmem_limit_bytes=VMEM_LIMIT),
    )(cols, counts, tile_values, x_tiles)


def aggregate_transposed(tile_values, cols, counts, g_tiles, col_tiles):
    row_tiles, slots, tile, _ = tile_values.shape
    width = g_tiles.shape[-1]
    return pl.pallas_call(
        backward_kernel,
        out_shape=jax.ShapeDtypeStruct((col_tiles, tile, width), jnp.bfloat16),
        grid_spec=pltpu.PrefetchScalarGridSpec(
            num_scalar_prefetch=2,
            grid=(row_tiles // GROUP,),
            in_specs=[
                pl.BlockSpec((GROUP, slots, tile, tile), lambda t, c, n: (t, 0, 0, 0)),
                pl.BlockSpec((GROUP, tile, width), lambda t, c, n: (t, 0, 0)),
            ],
            out_specs=pl.BlockSpec((col_tiles, tile, width), lambda t, c, n: (0, 0, 0)),
            scratch_shapes=[pltpu.VMEM((col_tiles, tile, width), jnp.float32)],
        ),
        compiler_params=pltpu.CompilerParams(vmem_limit_bytes=VMEM_LIMIT),
    )(cols, counts, tile_values, g_tiles)


def gather_over(x, axis):
    size = lax.axis_size(axis)
    spread = jnp.broadcast_to(x[None], (size,) + x.shape)
    got = lax.all_to_all(spread, axis, 0, 0, tiled=True)
    return got.reshape((size * x.shape[0],) + x.shape[1:])


def sum_scatter_over(x, axis):
    size = lax.axis_size(axis)
    parts = x.reshape((size, x.shape[0] // size) + x.shape[1:])
    got = lax.all_to_all(parts, axis, 0, 0, tiled=True)
    return got.astype(jnp.float32).sum(axis=0)


def sum_kernel(x_ref, o_ref):
    o_ref[...] = jnp.sum(x_ref[...].astype(jnp.float32), axis=0).astype(o_ref.dtype)


def sum_parts(parts, rows_per_step=128):
    count, rows, width = parts.shape
    return pl.pallas_call(
        sum_kernel,
        out_shape=jax.ShapeDtypeStruct((rows, width), jnp.bfloat16),
        grid=(rows // rows_per_step,),
        in_specs=[pl.BlockSpec((count, rows_per_step, width), lambda i: (0, i, 0))],
        out_specs=pl.BlockSpec((rows_per_step, width), lambda i: (i, 0)),
    )(parts)


def dense_part(hidden, weight, bias, cotangent):
    preact = jnp.dot(hidden, weight, preferred_element_type=jnp.float32) + bias
    output = jax.nn.silu(preact).astype(jnp.bfloat16)
    sigmoid_value = jax.nn.sigmoid(preact)
    slope = sigmoid_value * (1.0 + preact * (1.0 - sigmoid_value))
    preact_grad = (cotangent.astype(jnp.float32) * slope).astype(jnp.bfloat16)
    weight_grad = lax.dot_general(
        hidden, preact_grad, (((0,), (0,)), ((), ())), preferred_element_type=jnp.float32
    )
    bias_grad = jnp.sum(preact_grad.astype(jnp.float32), axis=0)
    hidden_grad = lax.dot_general(
        preact_grad, weight, (((1,), (1,)), ((), ())), preferred_element_type=jnp.float32
    ).astype(jnp.bfloat16)
    return (output, weight_grad, bias_grad, hidden_grad)


def all_sum(weight_grad, bias_grad):
    axes = ("row", "col")
    devices = lax.axis_size("row") * lax.axis_size("col")
    width = weight_grad.shape[1]
    rows = weight_grad.shape[0] + 1
    per = -(-rows // devices)
    packed = jnp.concatenate(
        [weight_grad, bias_grad[None], jnp.zeros((per * devices - rows, width), jnp.float32)]
    )
    parts = lax.all_to_all(packed.reshape(devices, per, width), axes, 0, 0, tiled=True)
    summed = parts.sum(axis=0, keepdims=True)
    spread = jnp.broadcast_to(summed, (devices, per, width))
    back = lax.all_to_all(spread, axes, 0, 0, tiled=True).reshape(devices * per, width)
    return back[: rows - 1], back[rows - 1]


def per_device(features, tile_values, tile_cols, tile_counts, weight, bias, cotangent):
    node_dev, width = features.shape
    row_tiles, slot_count, tile_size, _ = tile_values.shape
    column_block = gather_over(features, "col")
    column_tiles = column_block.shape[0] // tile_size
    x_tiles = column_block.reshape(column_tiles, tile_size, width)
    live_counts = tile_counts[:, 0]

    partial_value = aggregate(tile_values, tile_cols, live_counts, x_tiles)
    partial_value = partial_value.reshape(row_tiles * tile_size, width)
    node_total = node_dev * lax.axis_size("row") * lax.axis_size("col")
    grad_scale = 1.0 / math.sqrt(node_total)
    own_rows = sum_scatter_over(partial_value, "row").astype(jnp.bfloat16)
    layer_out, weight_grad, bias_grad, hidden_grad = dense_part(own_rows, weight, bias, cotangent)
    weight_grad, bias_grad = all_sum(weight_grad * grad_scale, bias_grad * grad_scale)
    grad_block = gather_over(hidden_grad, "row")
    grad_tiles = grad_block.reshape(row_tiles, tile_size, width)

    summed = aggregate_transposed(tile_values, tile_cols, live_counts, grad_tiles, column_tiles)
    summed = summed.reshape(column_tiles * tile_size, width)
    col_parts = summed.reshape((lax.axis_size("col"), -1, width))
    feature_grad = sum_parts(lax.all_to_all(col_parts, "col", 0, 0, tiled=True))
    return (layer_out, feature_grad, weight_grad, bias_grad)


def solution(mesh):
    placed = (
        P(("row", "col"), None),
        P("col", "row", None, None),
        P("col", "row"),
        P("col", "row"),
        P(),
        P(),
        P(("col", "row"), None),
    )
    return jax.shard_map(
        per_device,
        mesh=mesh,
        in_specs=placed,
        out_specs=(P(("col", "row"), None), P(("row", "col"), None), P(), P()),
        check_vma=False,
    )
```

```python
import functools
import math

import jax
import jax.numpy as jnp
from jax import lax
from jax.experimental import pallas as pl
from jax.experimental.pallas import tpu as pltpu
from jax.sharding import PartitionSpec as P

VMEM_LIMIT = 60 * 1024 * 1024
GROUP = 4


def forward_kernel(cols_ref, counts_ref, a_ref, x_ref, o_ref):
    step = pl.program_id(0)
    group, slots = a_ref.shape[:2]
    last = x_ref.shape[0] - 1
    for u in range(group):
        t = step * group + u
        live = counts_ref[t]
        acc = None
        for s in range(slots):
            j = jnp.clip(cols_ref[t, s], 0, last)
            term = jnp.dot(a_ref[u, s], x_ref[j], preferred_element_type=jnp.float32)
            term = jnp.where(s < live, term, 0.0)
            acc = term if acc is None else acc + term
        o_ref[u] = acc.astype(o_ref.dtype)


def backward_kernel(cols_ref, counts_ref, a_ref, g_ref, o_ref, acc_ref):
    step = pl.program_id(0)
    group, slots = a_ref.shape[:2]
    last = acc_ref.shape[0] - 1

    @pl.when(step == 0)
    def _():
        acc_ref[...] = jnp.zeros_like(acc_ref)

    for u in range(group):
        t = step * group + u
        live = counts_ref[t]
        g = g_ref[u]
        terms = [
            lax.dot_general(
                a_ref[u, s], g, (((0,), (0,)), ((), ())), preferred_element_type=jnp.float32
            )
            for s in range(slots)
        ]
        for s in range(slots):
            j = jnp.clip(cols_ref[t, s], 0, last)
            acc_ref[j] += jnp.where(s < live, terms[s], 0.0)

    @pl.when(step == pl.num_programs(0) - 1)
    def _():
        def put(j, carry):
            o_ref[j] = acc_ref[j].astype(o_ref.dtype)
            return carry

        lax.fori_loop(0, acc_ref.shape[0], put, 0)


def aggregate(tile_values, cols, counts, x_tiles):
    row_tiles, slots, tile, _ = tile_values.shape
    col_tiles, _, width = x_tiles.shape
    return pl.pallas_call(
        forward_kernel,
        out_shape=jax.ShapeDtypeStruct((row_tiles, tile, width), jnp.bfloat16),
        grid_spec=pltpu.PrefetchScalarGridSpec(
            num_scalar_prefetch=2,
            grid=(row_tiles // GROUP,),
            in_specs=[
                pl.BlockSpec((GROUP, slots, tile, tile), lambda t, c, n: (t, 0, 0, 0)),
                pl.BlockSpec(
                    (col_tiles, tile, width),
                    lambda t, c, n: (0, 0, 0),
                    pipeline_mode=pl.Buffered(1),
                ),
            ],
            out_specs=pl.BlockSpec((GROUP, tile, width), lambda t, c, n: (t, 0, 0)),
        ),
        compiler_params=pltpu.CompilerParams(vmem_limit_bytes=VMEM_LIMIT),
    )(cols, counts, tile_values, x_tiles)


def aggregate_transposed(tile_values, cols, counts, g_tiles, col_tiles):
    row_tiles, slots, tile, _ = tile_values.shape
    width = g_tiles.shape[-1]
    return pl.pallas_call(
        backward_kernel,
        out_shape=jax.ShapeDtypeStruct((col_tiles, tile, width), jnp.bfloat16),
        grid_spec=pltpu.PrefetchScalarGridSpec(
            num_scalar_prefetch=2,
            grid=(row_tiles // GROUP,),
            in_specs=[
                pl.BlockSpec((GROUP, slots, tile, tile), lambda t, c, n: (t, 0, 0, 0)),
                pl.BlockSpec((GROUP, tile, width), lambda t, c, n: (t, 0, 0)),
            ],
            out_specs=pl.BlockSpec((col_tiles, tile, width), lambda t, c, n: (0, 0, 0)),
            scratch_shapes=[pltpu.VMEM((col_tiles, tile, width), jnp.float32)],
        ),
        compiler_params=pltpu.CompilerParams(vmem_limit_bytes=VMEM_LIMIT),
    )(cols, counts, tile_values, g_tiles)


def gather_over(x, axis):
    size = lax.axis_size(axis)
    spread = jnp.broadcast_to(x[None], (size,) + x.shape)
    got = lax.all_to_all(spread, axis, 0, 0, tiled=True)
    return got.reshape((size * x.shape[0],) + x.shape[1:])


def sum_scatter_over(x, axis):
    size = lax.axis_size(axis)
    parts = x.reshape((size, x.shape[0] // size) + x.shape[1:])
    got = lax.all_to_all(parts, axis, 0, 0, tiled=True)
    return got.astype(jnp.float32).sum(axis=0)


def dense_part(hidden, weight, bias, cotangent):
    preact = jnp.dot(hidden, weight, preferred_element_type=jnp.float32) + bias
    output = jax.nn.silu(preact).astype(jnp.bfloat16)
    sigmoid_value = jax.nn.sigmoid(preact)
    slope = sigmoid_value * (1.0 + preact * (1.0 - sigmoid_value))
    preact_grad = (cotangent.astype(jnp.float32) * slope).astype(jnp.bfloat16)
    weight_grad = lax.dot_general(
        hidden, preact_grad, (((0,), (0,)), ((), ())), preferred_element_type=jnp.float32
    )
    bias_grad = jnp.sum(preact_grad.astype(jnp.float32), axis=0)
    hidden_grad = lax.dot_general(
        preact_grad, weight, (((1,), (1,)), ((), ())), preferred_element_type=jnp.float32
    ).astype(jnp.bfloat16)
    return (output, weight_grad, bias_grad, hidden_grad)


def all_sum(weight_grad, bias_grad):
    axes = ("row", "col")
    devices = lax.axis_size("row") * lax.axis_size("col")
    width = weight_grad.shape[1]
    rows = weight_grad.shape[0] + 1
    per = -(-rows // devices)
    packed = jnp.concatenate(
        [weight_grad, bias_grad[None], jnp.zeros((per * devices - rows, width), jnp.float32)]
    )
    parts = lax.all_to_all(packed.reshape(devices, per, width), axes, 0, 0, tiled=True)
    summed = parts.sum(axis=0, keepdims=True)
    spread = jnp.broadcast_to(summed, (devices, per, width))
    back = lax.all_to_all(spread, axes, 0, 0, tiled=True).reshape(devices * per, width)
    return back[: rows - 1], back[rows - 1]


def per_device(features, tile_values, tile_cols, tile_counts, weight, bias, cotangent):
    node_dev, width = features.shape
    row_tiles, slot_count, tile_size, _ = tile_values.shape
    column_block = gather_over(features, "col")
    column_tiles = column_block.shape[0] // tile_size
    x_tiles = column_block.reshape(column_tiles, tile_size, width)
    live_counts = tile_counts[:, 0]

    partial_value = aggregate(tile_values, tile_cols, live_counts, x_tiles)
    partial_value = partial_value.reshape(row_tiles * tile_size, width)
    node_total = node_dev * lax.axis_size("row") * lax.axis_size("col")
    grad_scale = 1.0 / math.sqrt(node_total)
    own_rows = sum_scatter_over(partial_value, "row").astype(jnp.bfloat16)
    layer_out, weight_grad, bias_grad, hidden_grad = dense_part(own_rows, weight, bias, cotangent)
    weight_grad, bias_grad = all_sum(weight_grad * grad_scale, bias_grad * grad_scale)
    grad_block = gather_over(hidden_grad, "row")
    grad_block, weight_grad, bias_grad = lax.optimization_barrier((grad_block, weight_grad, bias_grad))
    grad_tiles = grad_block.reshape(row_tiles, tile_size, width)

    summed = aggregate_transposed(tile_values, tile_cols, live_counts, grad_tiles, column_tiles)
    summed = summed.reshape(column_tiles * tile_size, width)
    feature_grad = sum_scatter_over(summed, "col").astype(jnp.bfloat16)
    return (layer_out, feature_grad, weight_grad, bias_grad)


def solution(mesh):
    placed = (
        P(("row", "col"), None),
        P("col", "row", None, None),
        P("col", "row"),
        P("col", "row"),
        P(),
        P(),
        P(("col", "row"), None),
    )
    return jax.shard_map(
        per_device,
        mesh=mesh,
        in_specs=placed,
        out_specs=(P(("col", "row"), None), P(("row", "col"), None), P(), P()),
        check_vma=False,
    )
```

```python
import functools
import math

import jax
import jax.numpy as jnp
from jax import lax
from jax.experimental import pallas as pl
from jax.experimental.pallas import tpu as pltpu
from jax.sharding import PartitionSpec as P

VMEM_LIMIT = 60 * 1024 * 1024
GROUP = 4


def forward_kernel(cols_ref, counts_ref, a_ref, x_ref, o_ref):
    step = pl.program_id(0)
    group, slots = a_ref.shape[:2]
    last = x_ref.shape[0] - 1
    for u in range(group):
        t = step * group + u
        live = counts_ref[t]
        acc = None
        for s in range(slots):
            j = jnp.clip(cols_ref[t, s], 0, last)
            term = jnp.dot(a_ref[u, s], x_ref[j], preferred_element_type=jnp.float32)
            term = jnp.where(s < live, term, 0.0)
            acc = term if acc is None else acc + term
        o_ref[u] = acc.astype(o_ref.dtype)


def backward_kernel(cols_ref, counts_ref, a_ref, g_ref, o_ref, acc_ref):
    step = pl.program_id(0)
    group, slots = a_ref.shape[:2]
    last = acc_ref.shape[0] - 1

    @pl.when(step == 0)
    def _():
        acc_ref[...] = jnp.zeros_like(acc_ref)

    for u in range(group):
        t = step * group + u
        live = counts_ref[t]
        g = g_ref[u]
        terms = [
            lax.dot_general(
                a_ref[u, s], g, (((0,), (0,)), ((), ())), preferred_element_type=jnp.float32
            )
            for s in range(slots)
        ]
        for s in range(slots):
            j = jnp.clip(cols_ref[t, s], 0, last)
            acc_ref[j] += jnp.where(s < live, terms[s], 0.0)

    @pl.when(step == pl.num_programs(0) - 1)
    def _():
        def put(j, carry):
            o_ref[j] = acc_ref[j].astype(o_ref.dtype)
            return carry

        lax.fori_loop(0, acc_ref.shape[0], put, 0)


def aggregate(tile_values, cols, counts, x_tiles):
    row_tiles, slots, tile, _ = tile_values.shape
    col_tiles, _, width = x_tiles.shape
    return pl.pallas_call(
        forward_kernel,
        out_shape=jax.ShapeDtypeStruct((row_tiles, tile, width), jnp.bfloat16),
        grid_spec=pltpu.PrefetchScalarGridSpec(
            num_scalar_prefetch=2,
            grid=(row_tiles // GROUP,),
            in_specs=[
                pl.BlockSpec((GROUP, slots, tile, tile), lambda t, c, n: (t, 0, 0, 0)),
                pl.BlockSpec(
                    (col_tiles, tile, width),
                    lambda t, c, n: (0, 0, 0),
                    pipeline_mode=pl.Buffered(1),
                ),
            ],
            out_specs=pl.BlockSpec((GROUP, tile, width), lambda t, c, n: (t, 0, 0)),
        ),
        compiler_params=pltpu.CompilerParams(vmem_limit_bytes=VMEM_LIMIT),
    )(cols, counts, tile_values, x_tiles)


def aggregate_transposed(tile_values, cols, counts, g_tiles, col_tiles):
    row_tiles, slots, tile, _ = tile_values.shape
    width = g_tiles.shape[-1]
    return pl.pallas_call(
        backward_kernel,
        out_shape=jax.ShapeDtypeStruct((col_tiles, tile, width), jnp.bfloat16),
        grid_spec=pltpu.PrefetchScalarGridSpec(
            num_scalar_prefetch=2,
            grid=(row_tiles // GROUP,),
            in_specs=[
                pl.BlockSpec((GROUP, slots, tile, tile), lambda t, c, n: (t, 0, 0, 0)),
                pl.BlockSpec((GROUP, tile, width), lambda t, c, n: (t, 0, 0)),
            ],
            out_specs=pl.BlockSpec((col_tiles, tile, width), lambda t, c, n: (0, 0, 0)),
            scratch_shapes=[pltpu.VMEM((col_tiles, tile, width), jnp.float32)],
        ),
        compiler_params=pltpu.CompilerParams(vmem_limit_bytes=VMEM_LIMIT),
    )(cols, counts, tile_values, g_tiles)


def gather_over(x, axis):
    size = lax.axis_size(axis)
    spread = jnp.broadcast_to(x[None], (size,) + x.shape)
    got = lax.all_to_all(spread, axis, 0, 0, tiled=True)
    return got.reshape((size * x.shape[0],) + x.shape[1:])


def sum_scatter_over(x, axis):
    size = lax.axis_size(axis)
    parts = x.reshape((size, x.shape[0] // size) + x.shape[1:])
    got = lax.all_to_all(parts, axis, 0, 0, tiled=True)
    return got.astype(jnp.float32).sum(axis=0)


def dense_part(hidden, weight, bias, cotangent):
    preact = jnp.dot(hidden, weight, preferred_element_type=jnp.float32) + bias
    output = jax.nn.silu(preact).astype(jnp.bfloat16)
    sigmoid_value = jax.nn.sigmoid(preact)
    slope = sigmoid_value * (1.0 + preact * (1.0 - sigmoid_value))
    preact_grad = (cotangent.astype(jnp.float32) * slope).astype(jnp.bfloat16)
    weight_grad = lax.dot_general(
        hidden, preact_grad, (((0,), (0,)), ((), ())), preferred_element_type=jnp.float32
    )
    bias_grad = jnp.sum(preact_grad.astype(jnp.float32), axis=0)
    hidden_grad = lax.dot_general(
        preact_grad, weight, (((1,), (1,)), ((), ())), preferred_element_type=jnp.float32
    ).astype(jnp.bfloat16)
    return (output, weight_grad, bias_grad, hidden_grad)


def split_wide(v):
    high = v.astype(jnp.bfloat16)
    low = (v - high.astype(jnp.float32)).astype(jnp.bfloat16)
    return high, low


def per_device(features, tile_values, tile_cols, tile_counts, weight, bias, cotangent):
    node_dev, width = features.shape
    row_tiles, slot_count, tile_size, _ = tile_values.shape
    n_row, n_col = lax.axis_size("row"), lax.axis_size("col")
    column_block = gather_over(features, "col")
    column_tiles = column_block.shape[0] // tile_size
    x_tiles = column_block.reshape(column_tiles, tile_size, width)
    live_counts = tile_counts[:, 0]

    partial_value = aggregate(tile_values, tile_cols, live_counts, x_tiles)
    partial_value = partial_value.reshape(row_tiles * tile_size, width)
    node_total = node_dev * n_row * n_col
    grad_scale = 1.0 / math.sqrt(node_total)
    own_rows = sum_scatter_over(partial_value, "row").astype(jnp.bfloat16)
    layer_out, weight_grad, bias_grad, hidden_grad = dense_part(own_rows, weight, bias, cotangent)

    terms = jnp.concatenate([weight_grad, bias_grad[None]]) * grad_scale
    rows = terms.shape[0]
    piece = -(-rows // n_col)
    terms = jnp.concatenate([terms, jnp.zeros((piece * n_col - rows, width), jnp.float32)])
    high, low = split_wide(terms)
    payload = jnp.concatenate([hidden_grad, high, low])
    got = lax.all_to_all(
        jnp.broadcast_to(payload[None], (n_row,) + payload.shape), "row", 0, 0, tiled=True
    )
    grad_block = got[:, :node_dev].reshape(n_row * node_dev, width)
    kept = piece * n_col
    row_sum = (
        got[:, node_dev : node_dev + kept].astype(jnp.float32)
        + got[:, node_dev + kept :].astype(jnp.float32)
    ).sum(axis=0)
    grad_tiles = grad_block.reshape(row_tiles, tile_size, width)

    summed = aggregate_transposed(tile_values, tile_cols, live_counts, grad_tiles, column_tiles)
    parts = summed.reshape(n_col, -1, width)
    chunk = parts.shape[1]
    high, low = split_wide(row_sum)
    payload = jnp.concatenate(
        [parts, high.reshape(n_col, piece, width), low.reshape(n_col, piece, width)], axis=1
    )
    got = lax.all_to_all(payload, "col", 0, 0, tiled=True)
    feature_grad = got[:, :chunk].astype(jnp.float32).sum(axis=0).astype(jnp.bfloat16)
    own_piece = (
        got[:, chunk : chunk + piece].astype(jnp.float32)
        + got[:, chunk + piece :].astype(jnp.float32)
    ).sum(axis=0)
    total = lax.all_to_all(
        jnp.broadcast_to(own_piece[None], (n_col, piece, width)), "col", 0, 0, tiled=True
    ).reshape(n_col * piece, width)
    return (layer_out, feature_grad, total[: rows - 1], total[rows - 1])


def solution(mesh):
    placed = (
        P(("row", "col"), None),
        P("col", "row", None, None),
        P("col", "row"),
        P("col", "row"),
        P(),
        P(),
        P(("col", "row"), None),
    )
    return jax.shard_map(
        per_device,
        mesh=mesh,
        in_specs=placed,
        out_specs=(P(("col", "row"), None), P(("row", "col"), None), P(), P()),
        check_vma=False,
    )
```

```python
import functools
import math

import jax
import jax.numpy as jnp
from jax import lax
from jax.experimental import pallas as pl
from jax.experimental.pallas import tpu as pltpu
from jax.sharding import PartitionSpec as P

VMEM_LIMIT = 60 * 1024 * 1024
GROUP = 4


def forward_kernel(cols_ref, counts_ref, a_ref, x_ref, o_ref):
    step = pl.program_id(0)
    group, slots = a_ref.shape[:2]
    last = x_ref.shape[0] - 1
    for u in range(group):
        t = step * group + u
        live = counts_ref[t]
        acc = None
        for s in range(slots):
            j = jnp.clip(cols_ref[t, s], 0, last)
            term = jnp.dot(a_ref[u, s], x_ref[j], preferred_element_type=jnp.float32)
            term = jnp.where(s < live, term, 0.0)
            acc = term if acc is None else acc + term
        o_ref[u] = acc.astype(o_ref.dtype)


def backward_kernel(cols_ref, counts_ref, a_ref, g_ref, o_ref, acc_ref):
    step = pl.program_id(0)
    group, slots = a_ref.shape[:2]
    last = acc_ref.shape[0] - 1

    @pl.when(step == 0)
    def _():
        acc_ref[...] = jnp.zeros_like(acc_ref)

    for u in range(group):
        t = step * group + u
        live = counts_ref[t]
        g = g_ref[u]
        terms = [
            lax.dot_general(
                a_ref[u, s], g, (((0,), (0,)), ((), ())), preferred_element_type=jnp.float32
            )
            for s in range(slots)
        ]
        for s in range(slots):
            j = jnp.clip(cols_ref[t, s], 0, last)
            acc_ref[j] += jnp.where(s < live, terms[s], 0.0)

    @pl.when(step == pl.num_programs(0) - 1)
    def _():
        def put(j, carry):
            o_ref[j] = acc_ref[j].astype(o_ref.dtype)
            return carry

        lax.fori_loop(0, acc_ref.shape[0], put, 0)


def aggregate(tile_values, cols, counts, x_tiles):
    row_tiles, slots, tile, _ = tile_values.shape
    col_tiles, _, width = x_tiles.shape
    return pl.pallas_call(
        forward_kernel,
        out_shape=jax.ShapeDtypeStruct((row_tiles, tile, width), jnp.bfloat16),
        grid_spec=pltpu.PrefetchScalarGridSpec(
            num_scalar_prefetch=2,
            grid=(row_tiles // GROUP,),
            in_specs=[
                pl.BlockSpec((GROUP, slots, tile, tile), lambda t, c, n: (t, 0, 0, 0)),
                pl.BlockSpec(
                    (col_tiles, tile, width),
                    lambda t, c, n: (0, 0, 0),
                    pipeline_mode=pl.Buffered(1),
                ),
            ],
            out_specs=pl.BlockSpec((GROUP, tile, width), lambda t, c, n: (t, 0, 0)),
        ),
        compiler_params=pltpu.CompilerParams(vmem_limit_bytes=VMEM_LIMIT),
    )(cols, counts, tile_values, x_tiles)


def aggregate_transposed(tile_values, cols, counts, g_tiles, col_tiles):
    row_tiles, slots, tile, _ = tile_values.shape
    width = g_tiles.shape[-1]
    return pl.pallas_call(
        backward_kernel,
        out_shape=jax.ShapeDtypeStruct((col_tiles, tile, width), jnp.bfloat16),
        grid_spec=pltpu.PrefetchScalarGridSpec(
            num_scalar_prefetch=2,
            grid=(row_tiles // GROUP,),
            in_specs=[
                pl.BlockSpec((GROUP, slots, tile, tile), lambda t, c, n: (t, 0, 0, 0)),
                pl.BlockSpec((GROUP, tile, width), lambda t, c, n: (t, 0, 0)),
            ],
            out_specs=pl.BlockSpec((col_tiles, tile, width), lambda t, c, n: (0, 0, 0)),
            scratch_shapes=[pltpu.VMEM((col_tiles, tile, width), jnp.float32)],
        ),
        compiler_params=pltpu.CompilerParams(vmem_limit_bytes=VMEM_LIMIT),
    )(cols, counts, tile_values, g_tiles)


def gather_over(x, axis):
    size = lax.axis_size(axis)
    spread = jnp.broadcast_to(x[None], (size,) + x.shape)
    got = lax.all_to_all(spread, axis, 0, 0, tiled=True)
    return got.reshape((size * x.shape[0],) + x.shape[1:])


def sum_scatter_over(x, axis):
    size = lax.axis_size(axis)
    parts = x.reshape((size, x.shape[0] // size) + x.shape[1:])
    got = lax.all_to_all(parts, axis, 0, 0, tiled=True)
    return got.astype(jnp.float32).sum(axis=0)


def dense_part(hidden, weight, bias, cotangent):
    preact = jnp.dot(hidden, weight, preferred_element_type=jnp.float32) + bias
    output = jax.nn.silu(preact).astype(jnp.bfloat16)
    sigmoid_value = jax.nn.sigmoid(preact)
    slope = sigmoid_value * (1.0 + preact * (1.0 - sigmoid_value))
    preact_grad = (cotangent.astype(jnp.float32) * slope).astype(jnp.bfloat16)
    weight_grad = lax.dot_general(
        hidden, preact_grad, (((0,), (0,)), ((), ())), preferred_element_type=jnp.float32
    )
    bias_grad = jnp.sum(preact_grad.astype(jnp.float32), axis=0)
    hidden_grad = lax.dot_general(
        preact_grad, weight, (((1,), (1,)), ((), ())), preferred_element_type=jnp.float32
    ).astype(jnp.bfloat16)
    return (output, weight_grad, bias_grad, hidden_grad)


def per_device(features, tile_values, tile_cols, tile_counts, weight, bias, cotangent):
    node_dev, width = features.shape
    row_tiles, slot_count, tile_size, _ = tile_values.shape
    n_row, n_col = lax.axis_size("row"), lax.axis_size("col")
    column_block = gather_over(features, "col")
    column_tiles = column_block.shape[0] // tile_size
    x_tiles = column_block.reshape(column_tiles, tile_size, width)
    live_counts = tile_counts[:, 0]

    partial_value = aggregate(tile_values, tile_cols, live_counts, x_tiles)
    partial_value = partial_value.reshape(row_tiles * tile_size, width)
    node_total = node_dev * n_row * n_col
    grad_scale = 1.0 / math.sqrt(node_total)
    own_rows = sum_scatter_over(partial_value, "row").astype(jnp.bfloat16)
    layer_out, weight_grad, bias_grad, hidden_grad = dense_part(own_rows, weight, bias, cotangent)

    terms = jnp.concatenate([weight_grad, bias_grad[None]]) * grad_scale
    rows = terms.shape[0]
    piece = -(-rows // n_col)
    terms = jnp.concatenate([terms, jnp.zeros((piece * n_col - rows, width), jnp.float32)])
    payload = jnp.concatenate([hidden_grad, terms.astype(jnp.bfloat16)])
    got = lax.all_to_all(
        jnp.broadcast_to(payload[None], (n_row,) + payload.shape), "row", 0, 0, tiled=True
    )
    grad_block = got[:, :node_dev].reshape(n_row * node_dev, width)
    row_sum = got[:, node_dev:].astype(jnp.float32).sum(axis=0)
    grad_tiles = grad_block.reshape(row_tiles, tile_size, width)

    summed = aggregate_transposed(tile_values, tile_cols, live_counts, grad_tiles, column_tiles)
    parts = summed.reshape(n_col, -1, width)
    chunk = parts.shape[1]
    payload = jnp.concatenate(
        [parts, row_sum.astype(jnp.bfloat16).reshape(n_col, piece, width)], axis=1
    )
    got = lax.all_to_all(payload, "col", 0, 0, tiled=True)
    feature_grad = got[:, :chunk].astype(jnp.float32).sum(axis=0).astype(jnp.bfloat16)
    own_piece = got[:, chunk:].astype(jnp.float32).sum(axis=0)
    total = lax.all_to_all(
        jnp.broadcast_to(own_piece[None], (n_col, piece, width)), "col", 0, 0, tiled=True
    ).reshape(n_col * piece, width)
    return (layer_out, feature_grad, total[: rows - 1], total[rows - 1])


def solution(mesh):
    placed = (
        P(("row", "col"), None),
        P("col", "row", None, None),
        P("col", "row"),
        P("col", "row"),
        P(),
        P(),
        P(("col", "row"), None),
    )
    return jax.shard_map(
        per_device,
        mesh=mesh,
        in_specs=placed,
        out_specs=(P(("col", "row"), None), P(("row", "col"), None), P(), P()),
        check_vma=False,
    )
```

```python
import functools
import math

import jax
import jax.numpy as jnp
from jax import lax
from jax.experimental import pallas as pl
from jax.experimental.pallas import tpu as pltpu
from jax.sharding import PartitionSpec as P

VMEM_LIMIT = 60 * 1024 * 1024
GROUP = 4


def forward_kernel(cols_ref, counts_ref, a_ref, x_ref, o_ref):
    step = pl.program_id(0)
    group, slots = a_ref.shape[:2]
    last = x_ref.shape[0] - 1
    for u in range(group):
        t = step * group + u
        live = counts_ref[t]
        acc = None
        for s in range(slots):
            j = jnp.clip(cols_ref[t, s], 0, last)
            term = jnp.dot(a_ref[u, s], x_ref[j], preferred_element_type=jnp.float32)
            term = jnp.where(s < live, term, 0.0)
            acc = term if acc is None else acc + term
        o_ref[u] = acc.astype(o_ref.dtype)


def backward_kernel(cols_ref, counts_ref, a_ref, g_ref, w_ref, o_ref, acc_ref):
    step = pl.program_id(0)
    group, slots = a_ref.shape[:2]
    last = acc_ref.shape[0] - 1

    @pl.when(step == 0)
    def _():
        acc_ref[...] = jnp.zeros_like(acc_ref)

    for u in range(group):
        t = step * group + u
        live = counts_ref[t]
        g = g_ref[u]
        terms = [
            lax.dot_general(
                a_ref[u, s], g, (((0,), (0,)), ((), ())), preferred_element_type=jnp.float32
            )
            for s in range(slots)
        ]
        for s in range(slots):
            j = jnp.clip(cols_ref[t, s], 0, last)
            acc_ref[j] += jnp.where(s < live, terms[s], 0.0)

    @pl.when(step == pl.num_programs(0) - 1)
    def _():
        tile = acc_ref.shape[1]
        per = o_ref.shape[1] // tile

        def put(j, carry):
            at = pl.multiple_of((j % per) * tile, tile)
            o_ref[j // per, pl.ds(at, tile)] = acc_ref[j].astype(o_ref.dtype)
            return carry

        lax.fori_loop(0, acc_ref.shape[0], put, 0)
        o_ref[:, pl.ds(per * tile, w_ref.shape[1])] = w_ref[...]


def aggregate(tile_values, cols, counts, x_tiles):
    row_tiles, slots, tile, _ = tile_values.shape
    col_tiles, _, width = x_tiles.shape
    return pl.pallas_call(
        forward_kernel,
        out_shape=jax.ShapeDtypeStruct((row_tiles, tile, width), jnp.bfloat16),
        grid_spec=pltpu.PrefetchScalarGridSpec(
            num_scalar_prefetch=2,
            grid=(row_tiles // GROUP,),
            in_specs=[
                pl.BlockSpec((GROUP, slots, tile, tile), lambda t, c, n: (t, 0, 0, 0)),
                pl.BlockSpec(
                    (col_tiles, tile, width),
                    lambda t, c, n: (0, 0, 0),
                    pipeline_mode=pl.Buffered(1),
                ),
            ],
            out_specs=pl.BlockSpec((GROUP, tile, width), lambda t, c, n: (t, 0, 0)),
        ),
        compiler_params=pltpu.CompilerParams(vmem_limit_bytes=VMEM_LIMIT),
    )(cols, counts, tile_values, x_tiles)


def aggregate_transposed(tile_values, cols, counts, g_tiles, pieces, col_tiles, chunk):
    row_tiles, slots, tile, _ = tile_values.shape
    width = g_tiles.shape[-1]
    n_col, piece, _ = pieces.shape
    return pl.pallas_call(
        backward_kernel,
        out_shape=jax.ShapeDtypeStruct((n_col, chunk + piece, width), jnp.bfloat16),
        grid_spec=pltpu.PrefetchScalarGridSpec(
            num_scalar_prefetch=2,
            grid=(row_tiles // GROUP,),
            in_specs=[
                pl.BlockSpec((GROUP, slots, tile, tile), lambda t, c, n: (t, 0, 0, 0)),
                pl.BlockSpec((GROUP, tile, width), lambda t, c, n: (t, 0, 0)),
                pl.BlockSpec((n_col, piece, width), lambda t, c, n: (0, 0, 0)),
            ],
            out_specs=pl.BlockSpec((n_col, chunk + piece, width), lambda t, c, n: (0, 0, 0)),
            scratch_shapes=[pltpu.VMEM((col_tiles, tile, width), jnp.float32)],
        ),
        compiler_params=pltpu.CompilerParams(vmem_limit_bytes=VMEM_LIMIT),
    )(cols, counts, tile_values, g_tiles, pieces)


def gather_over(x, axis):
    size = lax.axis_size(axis)
    spread = jnp.broadcast_to(x[None], (size,) + x.shape)
    got = lax.all_to_all(spread, axis, 0, 0, tiled=True)
    return got.reshape((size * x.shape[0],) + x.shape[1:])


def sum_scatter_over(x, axis):
    size = lax.axis_size(axis)
    parts = x.reshape((size, x.shape[0] // size) + x.shape[1:])
    got = lax.all_to_all(parts, axis, 0, 0, tiled=True)
    return got.astype(jnp.float32).sum(axis=0)


def dense_part(hidden, weight, bias, cotangent):
    preact = jnp.dot(hidden, weight, preferred_element_type=jnp.float32) + bias
    output = jax.nn.silu(preact).astype(jnp.bfloat16)
    sigmoid_value = jax.nn.sigmoid(preact)
    slope = sigmoid_value * (1.0 + preact * (1.0 - sigmoid_value))
    preact_grad = (cotangent.astype(jnp.float32) * slope).astype(jnp.bfloat16)
    weight_grad = lax.dot_general(
        hidden, preact_grad, (((0,), (0,)), ((), ())), preferred_element_type=jnp.float32
    )
    bias_grad = jnp.sum(preact_grad.astype(jnp.float32), axis=0)
    hidden_grad = lax.dot_general(
        preact_grad, weight, (((1,), (1,)), ((), ())), preferred_element_type=jnp.float32
    ).astype(jnp.bfloat16)
    return (output, weight_grad, bias_grad, hidden_grad)


def per_device(features, tile_values, tile_cols, tile_counts, weight, bias, cotangent):
    node_dev, width = features.shape
    row_tiles, slot_count, tile_size, _ = tile_values.shape
    n_row, n_col = lax.axis_size("row"), lax.axis_size("col")
    column_block = gather_over(features, "col")
    column_tiles = column_block.shape[0] // tile_size
    x_tiles = column_block.reshape(column_tiles, tile_size, width)
    live_counts = tile_counts[:, 0]

    partial_value = aggregate(tile_values, tile_cols, live_counts, x_tiles)
    partial_value = partial_value.reshape(row_tiles * tile_size, width)
    node_total = node_dev * n_row * n_col
    grad_scale = 1.0 / math.sqrt(node_total)
    own_rows = sum_scatter_over(partial_value, "row").astype(jnp.bfloat16)
    layer_out, weight_grad, bias_grad, hidden_grad = dense_part(own_rows, weight, bias, cotangent)

    terms = jnp.concatenate([weight_grad, bias_grad[None]]) * grad_scale
    rows = terms.shape[0]
    piece = -(-rows // n_col)
    terms = jnp.concatenate([terms, jnp.zeros((piece * n_col - rows, width), jnp.float32)])
    payload = jnp.concatenate([hidden_grad, terms.astype(jnp.bfloat16)])
    got = lax.all_to_all(
        jnp.broadcast_to(payload[None], (n_row,) + payload.shape), "row", 0, 0, tiled=True
    )
    grad_block = got[:, :node_dev].reshape(n_row * node_dev, width)
    row_sum = got[:, node_dev:].astype(jnp.float32).sum(axis=0)
    grad_tiles = grad_block.reshape(row_tiles, tile_size, width)

    chunk = column_tiles * tile_size // n_col
    pieces = row_sum.astype(jnp.bfloat16).reshape(n_col, piece, width)
    payload = aggregate_transposed(
        tile_values, tile_cols, live_counts, grad_tiles, pieces, column_tiles, chunk
    )
    got = lax.all_to_all(payload, "col", 0, 0, tiled=True)
    feature_grad = got[:, :chunk].astype(jnp.float32).sum(axis=0).astype(jnp.bfloat16)
    own_piece = got[:, chunk:].astype(jnp.float32).sum(axis=0)
    total = lax.all_to_all(
        jnp.broadcast_to(own_piece[None], (n_col, piece, width)), "col", 0, 0, tiled=True
    ).reshape(n_col * piece, width)
    return (layer_out, feature_grad, total[: rows - 1], total[rows - 1])


def solution(mesh):
    placed = (
        P(("row", "col"), None),
        P("col", "row", None, None),
        P("col", "row"),
        P("col", "row"),
        P(),
        P(),
        P(("col", "row"), None),
    )
    return jax.shard_map(
        per_device,
        mesh=mesh,
        in_specs=placed,
        out_specs=(P(("col", "row"), None), P(("row", "col"), None), P(), P()),
        check_vma=False,
    )
```

```python
import functools
import math

import jax
import jax.numpy as jnp
from jax import lax
from jax.experimental import pallas as pl
from jax.experimental.pallas import tpu as pltpu
from jax.sharding import PartitionSpec as P

VMEM_LIMIT = 60 * 1024 * 1024
GROUP = 4


def forward_kernel(cols_ref, counts_ref, a_ref, x_ref, o_ref):
    step = pl.program_id(0)
    group, slots = a_ref.shape[:2]
    last = x_ref.shape[0] - 1
    for u in range(group):
        t = step * group + u
        live = counts_ref[t]
        acc = None
        for s in range(slots):
            j = jnp.clip(cols_ref[t, s], 0, last)
            term = jnp.dot(a_ref[u, s], x_ref[j], preferred_element_type=jnp.float32)
            term = jnp.where(s < live, term, 0.0)
            acc = term if acc is None else acc + term
        o_ref[u] = acc.astype(o_ref.dtype)


def backward_kernel(cols_ref, counts_ref, a_ref, g_ref, w_ref, o_ref, acc_ref):
    step = pl.program_id(0)
    group, slots = a_ref.shape[:2]
    last = acc_ref.shape[0] - 1

    @pl.when(step == 0)
    def _():
        acc_ref[...] = jnp.zeros_like(acc_ref)

    for u in range(group):
        t = step * group + u
        live = counts_ref[t]
        g = g_ref[u]
        terms = [
            lax.dot_general(
                a_ref[u, s], g, (((0,), (0,)), ((), ())), preferred_element_type=jnp.float32
            )
            for s in range(slots)
        ]
        for s in range(slots):
            j = jnp.clip(cols_ref[t, s], 0, last)
            acc_ref[j] += jnp.where(s < live, terms[s], 0.0)

    @pl.when(step == pl.num_programs(0) - 1)
    def _():
        tile = acc_ref.shape[1]
        per = o_ref.shape[1] // tile

        def put(j, carry):
            at = pl.multiple_of((j % per) * tile, tile)
            o_ref[j // per, pl.ds(at, tile)] = acc_ref[j].astype(o_ref.dtype)
            return carry

        lax.fori_loop(0, acc_ref.shape[0], put, 0)
        o_ref[:, pl.ds(per * tile, w_ref.shape[1])] = w_ref[...]


def aggregate(tile_values, cols, counts, x_tiles):
    row_tiles, slots, tile, _ = tile_values.shape
    col_tiles, _, width = x_tiles.shape
    return pl.pallas_call(
        forward_kernel,
        out_shape=jax.ShapeDtypeStruct((row_tiles, tile, width), jnp.bfloat16),
        grid_spec=pltpu.PrefetchScalarGridSpec(
            num_scalar_prefetch=2,
            grid=(row_tiles // GROUP,),
            in_specs=[
                pl.BlockSpec((GROUP, slots, tile, tile), lambda t, c, n: (t, 0, 0, 0)),
                pl.BlockSpec(
                    (col_tiles, tile, width),
                    lambda t, c, n: (0, 0, 0),
                    pipeline_mode=pl.Buffered(1),
                ),
            ],
            out_specs=pl.BlockSpec((GROUP, tile, width), lambda t, c, n: (t, 0, 0)),
        ),
        compiler_params=pltpu.CompilerParams(vmem_limit_bytes=VMEM_LIMIT),
    )(cols, counts, tile_values, x_tiles)


def aggregate_transposed(tile_values, cols, counts, g_tiles, pieces, col_tiles, chunk):
    row_tiles, slots, tile, _ = tile_values.shape
    width = g_tiles.shape[-1]
    n_col, piece, _ = pieces.shape
    return pl.pallas_call(
        backward_kernel,
        out_shape=jax.ShapeDtypeStruct((n_col, chunk + piece, width), jnp.bfloat16),
        grid_spec=pltpu.PrefetchScalarGridSpec(
            num_scalar_prefetch=2,
            grid=(row_tiles // GROUP,),
            in_specs=[
                pl.BlockSpec((GROUP, slots, tile, tile), lambda t, c, n: (t, 0, 0, 0)),
                pl.BlockSpec((GROUP, tile, width), lambda t, c, n: (t, 0, 0)),
                pl.BlockSpec((n_col, piece, width), lambda t, c, n: (0, 0, 0)),
            ],
            out_specs=pl.BlockSpec((n_col, chunk + piece, width), lambda t, c, n: (0, 0, 0)),
            scratch_shapes=[pltpu.VMEM((col_tiles, tile, width), jnp.float32)],
        ),
        compiler_params=pltpu.CompilerParams(vmem_limit_bytes=VMEM_LIMIT),
    )(cols, counts, tile_values, g_tiles, pieces)


def gather_over(x, axis):
    size = lax.axis_size(axis)
    spread = jnp.broadcast_to(x[None], (size,) + x.shape)
    got = lax.all_to_all(spread, axis, 0, 0, tiled=True)
    return got.reshape((size * x.shape[0],) + x.shape[1:])


def sum_scatter_over(x, axis):
    size = lax.axis_size(axis)
    parts = x.reshape((size, x.shape[0] // size) + x.shape[1:])
    got = lax.all_to_all(parts, axis, 0, 0, tiled=True)
    return got.astype(jnp.float32).sum(axis=0)


def sum_kernel(x_ref, o_ref):
    o_ref[...] = x_ref[0].astype(jnp.float32)

    def add(i, carry):
        o_ref[...] += x_ref[i].astype(jnp.float32)
        return carry

    lax.fori_loop(1, x_ref.shape[0], add, 0)


def sum_parts(parts):
    count, rows, width = parts.shape
    return pl.pallas_call(
        sum_kernel,
        out_shape=jax.ShapeDtypeStruct((rows, width), jnp.float32),
        in_specs=[pl.BlockSpec(memory_space=pltpu.VMEM)],
        out_specs=pl.BlockSpec(memory_space=pltpu.VMEM),
        compiler_params=pltpu.CompilerParams(vmem_limit_bytes=VMEM_LIMIT),
    )(parts)


def dense_part(hidden, weight, bias, cotangent):
    preact = jnp.dot(hidden, weight, preferred_element_type=jnp.float32) + bias
    output = jax.nn.silu(preact).astype(jnp.bfloat16)
    sigmoid_value = jax.nn.sigmoid(preact)
    slope = sigmoid_value * (1.0 + preact * (1.0 - sigmoid_value))
    preact_grad = (cotangent.astype(jnp.float32) * slope).astype(jnp.bfloat16)
    weight_grad = lax.dot_general(
        hidden, preact_grad, (((0,), (0,)), ((), ())), preferred_element_type=jnp.float32
    )
    bias_grad = jnp.sum(preact_grad.astype(jnp.float32), axis=0)
    hidden_grad = lax.dot_general(
        preact_grad, weight, (((1,), (1,)), ((), ())), preferred_element_type=jnp.float32
    ).astype(jnp.bfloat16)
    return (output, weight_grad, bias_grad, hidden_grad)


def per_device(features, tile_values, tile_cols, tile_counts, weight, bias, cotangent):
    node_dev, width = features.shape
    row_tiles, slot_count, tile_size, _ = tile_values.shape
    n_row, n_col = lax.axis_size("row"), lax.axis_size("col")
    column_block = gather_over(features, "col")
    column_tiles = column_block.shape[0] // tile_size
    x_tiles = column_block.reshape(column_tiles, tile_size, width)
    live_counts = tile_counts[:, 0]

    partial_value = aggregate(tile_values, tile_cols, live_counts, x_tiles)
    partial_value = partial_value.reshape(row_tiles * tile_size, width)
    node_total = node_dev * n_row * n_col
    grad_scale = 1.0 / math.sqrt(node_total)
    own_rows = sum_scatter_over(partial_value, "row").astype(jnp.bfloat16)
    layer_out, weight_grad, bias_grad, hidden_grad = dense_part(own_rows, weight, bias, cotangent)

    terms = jnp.concatenate([weight_grad, bias_grad[None]]) * grad_scale
    rows = terms.shape[0]
    piece = -(-rows // n_col)
    terms = jnp.concatenate([terms, jnp.zeros((piece * n_col - rows, width), jnp.float32)])
    payload = jnp.concatenate([hidden_grad, terms.astype(jnp.bfloat16)])
    got = lax.all_to_all(
        jnp.broadcast_to(payload[None], (n_row,) + payload.shape), "row", 0, 0, tiled=True
    )
    grad_block = got[:, :node_dev].reshape(n_row * node_dev, width)
    row_sum = got[:, node_dev:].astype(jnp.float32).sum(axis=0)
    grad_tiles = grad_block.reshape(row_tiles, tile_size, width)

    chunk = column_tiles * tile_size // n_col
    pieces = row_sum.astype(jnp.bfloat16).reshape(n_col, piece, width)
    payload = aggregate_transposed(
        tile_values, tile_cols, live_counts, grad_tiles, pieces, column_tiles, chunk
    )
    got = lax.all_to_all(payload, "col", 0, 0, tiled=True)
    col_sum = sum_parts(got)
    feature_grad = col_sum[:chunk].astype(jnp.bfloat16)
    own_piece = col_sum[chunk:]
    total = lax.all_to_all(
        jnp.broadcast_to(own_piece[None], (n_col, piece, width)), "col", 0, 0, tiled=True
    ).reshape(n_col * piece, width)
    return (layer_out, feature_grad, total[: rows - 1], total[rows - 1])


def solution(mesh):
    placed = (
        P(("row", "col"), None),
        P("col", "row", None, None),
        P("col", "row"),
        P("col", "row"),
        P(),
        P(),
        P(("col", "row"), None),
    )
    return jax.shard_map(
        per_device,
        mesh=mesh,
        in_specs=placed,
        out_specs=(P(("col", "row"), None), P(("row", "col"), None), P(), P()),
        check_vma=False,
    )
```
